128 devices in a mesh: dom: 64 (over x, z, y), feat: 2 (over core).
Axes of the slice: x: 4, y: 4, z: 4, core: 2. Of those that a mesh axis runs over, the one named last changes fastest.
Arguments:
- features: bfloat16 [262144, 256], P('dom', 'feat')
- send_rows: int32 [64, 64, 128], P('dom'), may hold values from 0 to 4095
- send_counts: int32 [64, 64], P('dom'), may hold values from 0 to 128, as said below
- tile_src: int32 [2048, 24], P('dom'), may hold values from 0 to 95
- edge_codes: int32 [2048, 24, 512], P('dom'), may hold values from 0 to 16383
- degrees: int32 [262144], P('dom'), may hold values from 16 to 511
- w_self: bfloat16 [256, 256], replicated, may hold values from -0.375 to 0.375
- w_neigh: bfloat16 [256, 256], replicated, may hold values from -0.375 to 0.375
- gamma: float32 [256], P('feat'), may hold values from 0.1 to 1.9
- beta: float32 [256], P('feat'), may hold values from -4 to 4
Outputs:
- node_out: bfloat16 [262144, 256], P('dom', 'feat')
The draws below stay inside these ranges and needn't reach their ends.
Inputs may be any that keep to these rules, and one draw needn't show every extreme that they name: `send_rows`: entries are rows of the sending partition; repeats may occur. send_counts[d, d] is 0, and send_counts[d, (d + 1) % 64] is 128 for every d. `tile_src`: source tile numbers below 32 are the partition's own tiles; the rest are received rows. `edge_codes`: A code i * 128 + j is an edge from column j of the source tile to row i of the destination tile; repeated codes count as several edges.
All inputs are finite; a program needn't handle non-finite values.
Results may differ from the reference program's by a relative error of at most 0.0007.
Values may be sent and summed in bfloat16 or wider, within the bound.
No kernel may reach another device: no remote copies, remote signals or barrier semaphores. Data moves between devices by JAX's collectives and lax.ppermute only.
A program may use at most 64 MiB of HBM per device.

```python
import math
import jax
import jax.numpy as jnp
from jax import lax

C = 256
ROWS_DEV = 4096
TILE = 128
K = 24
SEND = 128
EDGES = 512
NODES = 262144
ST = 96
N_DOM = 64


def draw_features(key, part):
    keys = jax.random.split(key, 4)
    position = jnp.arange(NODES, dtype=jnp.float32) / NODES
    row_spread = jnp.exp(jax.random.uniform(keys[0], (NODES, 1), jnp.float32) * math.log(10.0)) / math.sqrt(10.0)
    col_spread = jnp.exp(jax.random.uniform(keys[1], (1, C), jnp.float32) * math.log(10.0)) / math.sqrt(10.0)
    offsets = jax.random.uniform(keys[2], (1, C), jnp.float32, -1.0, 1.0)
    row_ramp = 1.0 + 2.0 * position
    noise = jax.random.normal(keys[3], (NODES, C), jnp.float32)
    value = row_ramp[:, None] * row_spread * col_spread * (noise + offsets)
    return value.astype(jnp.bfloat16)


def draw_send_counts(key, part):
    counts = jax.random.randint(key, (N_DOM, N_DOM), SEND // 4, SEND + 1, dtype=jnp.int32)
    row_ids = jnp.arange(N_DOM, dtype=jnp.int32)[:, None]
    col_ids = jnp.arange(N_DOM, dtype=jnp.int32)[None, :]
    counts = jnp.where(col_ids == (row_ids + 1) % N_DOM, SEND, counts)
    counts = jnp.where(col_ids == row_ids, 0, counts)
    return counts.astype(jnp.int32)


def draw_degrees(key, part):
    first, second = jax.random.split(key)
    exponent = jax.random.randint(first, (NODES,), 4, 9, dtype=jnp.int32)
    base_value = jnp.left_shift(jnp.ones((NODES,), jnp.int32), exponent)
    extra = jax.random.randint(second, (NODES,), 0, base_value, dtype=jnp.int32)
    return (base_value + extra).astype(jnp.int32)


def touch_ends(values, rng, smallest, top_value):
    index_at = [jax.random.randint(jax.random.fold_in(rng, axis), (), 0, length) for axis, length in enumerate(values.shape)]
    main_axis = values.shape.index(max(values.shape))
    next_to = index_at[:main_axis] + [(index_at[main_axis] + 1) % values.shape[main_axis]] + index_at[main_axis + 1:]
    return values.at[tuple(index_at)].set(smallest).at[tuple(next_to)].set(top_value)


def levels(key, shape, shards, low, top_value):
    gain, own = 1.0, jax.random.fold_in(key, 6)
    for dim, shards_of in shards:
        heights = jnp.exp(jax.random.uniform(jax.random.fold_in(own, dim), (shards_of,), jnp.float32, low / len(shards), top_value / len(shards)))
        gain = gain * jnp.repeat(heights, shape[dim] // shards_of).reshape([-1 if axis == dim else 1 for axis in range(len(shape))])
    return gain


def gaussian(key, dims, scale, bound, pieces=(), kind=jnp.bfloat16):
    result = jax.random.normal(key, dims, jnp.float32) * scale
    if len(pieces) > 0:
        result = levels(key, dims, pieces, -0.22, 0.18) * result
    return jnp.clip(result, min=-bound, max=bound).astype(kind)


def setup_inputs(seed: int = 0) -> dict:
    arg_keys = jax.random.split(jax.random.key(seed), 11)
    features = draw_features(jax.random.fold_in(arg_keys[10], 71), 0)
    send_rows = touch_ends(jax.random.randint(arg_keys[1], (N_DOM, N_DOM, SEND), 0, ROWS_DEV), jax.random.fold_in(arg_keys[1], 1), 0, ROWS_DEV - 1).astype(jnp.int32)
    send_counts = draw_send_counts(jax.random.fold_in(arg_keys[10], 71), 0)
    tile_src = touch_ends(jax.random.randint(arg_keys[3], (NODES // TILE, K), 0, ST), jax.random.fold_in(arg_keys[3], 1), 0, ST - 1).astype(jnp.int32)
    edge_codes = touch_ends(jax.random.randint(arg_keys[4], (NODES // TILE, K, EDGES), 0, TILE * TILE), jax.random.fold_in(arg_keys[4], 1), 0, (TILE * TILE) - 1).astype(jnp.int32)
    degrees = draw_degrees(jax.random.fold_in(arg_keys[10], 71), 0)
    w_self = gaussian(arg_keys[6], (C, C), C ** -0.5, 0.375)
    w_neigh = gaussian(arg_keys[7], (C, C), C ** -0.5, 0.375)
    gamma = jnp.clip(1.0 + 0.18 * jax.random.normal(arg_keys[8], (C,), jnp.float32), 0.1, 1.9)
    beta = gaussian(arg_keys[9], (C,), 1.0, 4.0, ((0, 2),), jnp.float32)
    return {"features": features, "send_rows": send_rows, "send_counts": send_counts, "tile_src": tile_src, "edge_codes": edge_codes, "degrees": degrees, "w_self": w_self, "w_neigh": w_neigh, "gamma": gamma, "beta": beta}


def tile_counts(codes):
    return jnp.zeros((TILE * TILE,), jnp.float32).at[codes].add(1.0)

def group_sum(codes, indices, sources):
    group_size, per_tile = indices.shape
    flat = codes.reshape(group_size * per_tile, -1)
    adjacency = jax.vmap(tile_counts)(flat).reshape(group_size, per_tile, TILE, TILE)
    picked = sources[indices].astype(jnp.float32)
    return jnp.einsum('gkij,gkjc->gic', adjacency, picked)

def reference(features, send_rows, send_counts, tile_src, edge_codes, degrees, w_self, w_neigh, gamma, beta):
    node_count, channels = features.shape
    row_count = node_count // N_DOM
    dest_tiles = row_count // TILE
    group_size = math.gcd(dest_tiles, 8)
    edge_count = edge_codes.shape[2]
    blocks = features.reshape(N_DOM, row_count, channels)
    slot_ids = jnp.arange(SEND, dtype=jnp.int32)

    def one_part(part_id):
        slot_rows = send_rows[:, part_id, :]
        counts_in = send_counts[:, part_id]
        picked = jax.vmap(lambda block, rows_of: block[rows_of])(blocks, slot_rows)
        live = slot_ids[None, :] < counts_in[:, None]
        halo = jnp.where(live[:, :, None], picked, jnp.zeros_like(picked)).astype(jnp.bfloat16)
        own = lax.dynamic_index_in_dim(blocks, part_id, 0, keepdims=False)
        sources = jnp.concatenate([own, halo.reshape(-1, channels)], axis=0).reshape(-1, TILE, channels)
        start = (part_id * dest_tiles).astype(jnp.int32)
        codes = lax.dynamic_slice_in_dim(edge_codes, start, dest_tiles, 0)
        indices = lax.dynamic_slice_in_dim(tile_src, start, dest_tiles, 0)
        codes = codes.reshape(dest_tiles // group_size, group_size, K, edge_count)
        indices = indices.reshape(dest_tiles // group_size, group_size, K)
        sums = lax.map(lambda pair: group_sum(pair[0], pair[1], sources), (codes, indices))
        sums = sums.reshape(row_count, channels)
        degree_part = lax.dynamic_slice_in_dim(degrees, (part_id * row_count).astype(jnp.int32), row_count, 0)
        return (sums / degree_part.astype(jnp.float32)[:, None]).astype(jnp.bfloat16)
    agg = lax.map(one_part, jnp.arange(N_DOM, dtype=jnp.int32)).reshape(node_count, channels)
    pre = jnp.dot(features, w_self, preferred_element_type=jnp.float32) + jnp.dot(agg, w_neigh, preferred_element_type=jnp.float32)
    mean = lax.optimization_barrier(jnp.mean(pre, axis=0))
    var = lax.optimization_barrier(jnp.mean((pre - mean) * (pre - mean), axis=0))
    normed = gamma * (pre - mean) / jnp.sqrt(var + 1e-05) + beta
    return jnp.maximum(normed, 0.0).astype(jnp.bfloat16)
```

```python
import jax
import jax.numpy as jnp
from jax import lax
from jax.experimental import pallas as pl
from jax.experimental.pallas import tpu as pltpu
from jax.sharding import PartitionSpec as P

TILE = 128
PEERS_STEP = 8
EPS = 1e-05
BF16 = jnp.bfloat16
F32 = jnp.float32


def params(mib, axes=1):
    return pltpu.CompilerParams(
        dimension_semantics=("arbitrary",) * axes, vmem_limit_bytes=mib * 2**20
    )


def pick_kernel(idx_ref, own_ref, other_ref, out_ref, table):
    half = own_ref.shape[1]
    chunks = own_ref.shape[0] // TILE

    @pl.when(pl.program_id(0) == 0)
    def _():
        table[:, :half] = own_ref[...]
        table[:, half:] = other_ref[...]

    slots, peers = idx_ref.shape[1:]
    cols = idx_ref[0]
    lane = lax.broadcasted_iota(jnp.int32, (slots, TILE), 1)
    rows = []
    for p in range(peers):
        col = jnp.broadcast_to(cols[:, p : p + 1], (slots, TILE))
        low = jnp.where((col & (TILE - 1)) == lane, 1.0, 0.0).astype(BF16)
        high = (col >> 7).astype(F32).astype(BF16)
        zero = jnp.zeros_like(low)
        rows.append(
            jnp.concatenate(
                [jnp.where(high == jnp.asarray(c, BF16), low, zero) for c in range(chunks)],
                axis=1,
            )
        )
    hot = jnp.concatenate(rows, axis=0)
    picked = jnp.dot(hot, table[...], preferred_element_type=F32).astype(BF16)
    out_ref[...] = picked.reshape(out_ref.shape)


def pick_rows(idx, own, other):
    groups, slots, peers = idx.shape
    rows, half = own.shape
    return pl.pallas_call(
        pick_kernel,
        grid=(groups,),
        in_specs=[
            pl.BlockSpec((1, slots, peers), lambda g: (g, 0, 0)),
            pl.BlockSpec((rows, half), lambda g: (0, 0)),
            pl.BlockSpec((rows, half), lambda g: (0, 0)),
        ],
        out_specs=pl.BlockSpec((peers, slots, 2 * half), lambda g: (g, 0, 0)),
        out_shape=jax.ShapeDtypeStruct((groups * peers, slots, 2 * half), BF16),
        scratch_shapes=[pltpu.VMEM((rows, 2 * half), BF16)],
        compiler_params=params(40),
        name="pick_rows",
    )(idx, own, other)


def adjacency_kernel(core_ref, codes_ref, out_ref):
    per_tile, edges = codes_ref.shape[1:]
    ids = lax.broadcasted_iota(jnp.int32, (TILE, edges), 0).astype(F32).astype(BF16)
    one = jnp.ones((TILE, edges), BF16)
    zero = jnp.zeros((TILE, edges), BF16)

    def hot(values):
        spread = jnp.broadcast_to(values.astype(F32), (16, edges)).astype(BF16)
        spread = jnp.concatenate([spread] * (TILE // 16), axis=0)
        return jnp.where(spread == ids, one, zero)

    for k in range(per_tile):
        codes = codes_ref[0, k : k + 1, :]
        counts = lax.dot_general(
            hot(codes >> 7),
            hot(codes & (TILE - 1)),
            (((1,), (1,)), ((), ())),
            preferred_element_type=F32,
        )
        out_ref[0, :, k * TILE : (k + 1) * TILE] = counts.astype(BF16)


def adjacency(core, codes, tiles):
    _, per_tile, edges = codes.shape
    return pl.pallas_call(
        adjacency_kernel,
        grid_spec=pltpu.PrefetchScalarGridSpec(
            num_scalar_prefetch=1,
            grid=(tiles,),
            in_specs=[
                pl.BlockSpec(
                    (1, per_tile, edges), lambda t, core_ref: (core_ref[0] * tiles + t, 0, 0)
                )
            ],
            out_specs=pl.BlockSpec((1, TILE, per_tile * TILE), lambda t, core_ref: (t, 0, 0)),
        ),
        out_shape=jax.ShapeDtypeStruct((tiles, TILE, per_tile * TILE), BF16),
        compiler_params=params(40),
        cost_estimate=pl.CostEstimate(
            flops=2 * tiles * per_tile * TILE * TILE * edges * 2,
            transcendentals=0,
            bytes_accessed=tiles * per_tile * (TILE * TILE * 2 + edges * 4),
        ),
        name="adjacency",
    )(core, codes)


def aggregate_kernel(
    core_ref,
    tile_src_ref,
    adj_ref,
    deg_ref,
    weight_ref,
    own_ref,
    other_ref,
    mine_ref,
    sibling_ref,
    keep_ref,
    send_ref,
    sources,
    agg,
    sems,
):
    tiles, per_tile = tile_src_ref.shape
    tiles //= 2
    step = pl.program_id(0)
    core = core_ref[0]
    own_tiles = own_ref.shape[0]
    peers, slots, width = mine_ref.shape
    half = width // 2
    lo = pl.ds(0, half)
    hi = pl.ds(half, half)

    @pl.when(step == 0)
    def _():
        owned = pl.ds(0, own_tiles)
        halo = pl.ds(own_tiles, peers)
        here = pl.ds(pl.multiple_of(core * slots, slots), slots)
        there = pl.ds(pl.multiple_of((1 - core) * slots, slots), slots)
        copies = [
            pltpu.make_async_copy(own_ref, sources.at[owned, :, lo], sems.at[0]),
            pltpu.make_async_copy(other_ref, sources.at[owned, :, hi], sems.at[1]),
            pltpu.make_async_copy(mine_ref, sources.at[halo, here, :], sems.at[2]),
            pltpu.make_async_copy(
                sibling_ref.at[:, :, hi], sources.at[halo, there, lo], sems.at[3]
            ),
            pltpu.make_async_copy(
                sibling_ref.at[:, :, lo], sources.at[halo, there, hi], sems.at[4]
            ),
        ]
        for copy in copies:
            copy.start()
        for copy in copies:
            copy.wait()

    row = core * tiles + step
    total = jnp.zeros((TILE, width), F32)
    for k in range(0, per_tile, 2):
        pair = jnp.concatenate(
            [sources[tile_src_ref[row, k]], sources[tile_src_ref[row, k + 1]]], axis=0
        )
        total += jnp.dot(
            adj_ref[0, :, k * TILE : (k + 2) * TILE], pair, preferred_element_type=F32
        )
    degree = deg_ref[0].astype(F32)
    column = jnp.broadcast_to(degree, (8, TILE)).T[:, :1]
    mean_rows = (total / column).astype(BF16)
    both = jnp.concatenate([sources[row], mean_rows], axis=1)
    pre = jnp.dot(both, weight_ref[...], preferred_element_type=F32)
    keep_ref[...] = pre[:, :half]
    send_ref[...] = pre[:, half:]


def aggregate(core, tile_src, adj, degrees, weights, own, other, mine, sibling):
    tiles = adj.shape[0]
    width = mine.shape[2]
    half = width // 2
    rows = tiles * TILE
    source_tiles = own.shape[0] // TILE + mine.shape[0]
    own = own.reshape(-1, TILE, half)
    other = other.reshape(-1, TILE, half)
    anywhere = pl.BlockSpec(memory_space=pl.ANY)
    return pl.pallas_call(
        aggregate_kernel,
        grid_spec=pltpu.PrefetchScalarGridSpec(
            num_scalar_prefetch=2,
            grid=(tiles,),
            in_specs=[
                pl.BlockSpec((1,) + adj.shape[1:], lambda t, c, s: (t, 0, 0)),
                pl.BlockSpec((1, 1, TILE), lambda t, c, s: (c[0] * tiles + t, 0, 0)),
                pl.BlockSpec(weights.shape, lambda t, c, s: (0, 0)),
                anywhere,
                anywhere,
                anywhere,
                anywhere,
            ],
            out_specs=[pl.BlockSpec((TILE, half), lambda t, c, s: (t, 0))] * 2,
            scratch_shapes=[
                pltpu.VMEM((source_tiles, TILE, width), BF16),
                pltpu.VMEM((TILE, width), BF16),
                pltpu.SemaphoreType.DMA((5,)),
            ],
        ),
        out_shape=[jax.ShapeDtypeStruct((rows, half), F32)] * 2,
        compiler_params=params(40),
        name="aggregate",
    )(core, tile_src, adj, degrees, weights, own, other, mine, sibling)


def moments_kernel(keep_ref, got_ref, out_ref):
    count = keep_ref.shape[0] + got_ref.shape[0]
    keep = keep_ref[...]
    got = got_ref[...]
    total = jnp.sum(keep, axis=0, keepdims=True) + jnp.sum(got, axis=0, keepdims=True)
    mean = total / count
    spread = jnp.sum(jnp.square(keep - mean), axis=0, keepdims=True) + jnp.sum(
        jnp.square(got - mean), axis=0, keepdims=True
    )
    both = jnp.concatenate([total, spread], axis=0)
    out_ref[...] = jnp.broadcast_to(both[None], out_ref.shape)


def moments(keep, got, peers):
    return pl.pallas_call(
        moments_kernel,
        out_shape=jax.ShapeDtypeStruct((peers, 2, keep.shape[1]), F32),
        compiler_params=pltpu.CompilerParams(vmem_limit_bytes=40 * 2**20),
        name="moments",
    )(keep, got)


def normalise_kernel(core_ref, keep_ref, got_ref, parts_ref, gamma_ref, beta_ref, out_ref):
    rows = keep_ref.shape[0]
    count = float(2 * rows)
    parts = parts_ref[...]
    peers = parts.shape[0]
    totals = parts[:, 0, :]
    spreads = parts[:, 1, :]
    mean = jnp.sum(totals, axis=0, keepdims=True) / (count * peers)
    shift = totals / count - mean
    var = jnp.sum(spreads + count * shift * shift, axis=0, keepdims=True) / (count * peers)
    scale = gamma_ref[...] / jnp.sqrt(var + EPS)
    beta = beta_ref[...]
    here = pl.multiple_of(core_ref[0] * rows, rows)
    there = pl.multiple_of((1 - core_ref[0]) * rows, rows)
    out_ref[pl.ds(here, rows), :] = jnp.maximum(
        (keep_ref[...] - mean) * scale + beta, 0.0
    ).astype(BF16)
    out_ref[pl.ds(there, rows), :] = jnp.maximum(
        (got_ref[...] - mean) * scale + beta, 0.0
    ).astype(BF16)


def normalise(core, keep, got, parts, gamma, beta):
    rows, half = keep.shape
    whole = pl.BlockSpec(memory_space=pltpu.VMEM)
    return pl.pallas_call(
        normalise_kernel,
        in_specs=[pl.BlockSpec(memory_space=pltpu.SMEM)] + [whole] * 5,
        out_specs=whole,
        out_shape=jax.ShapeDtypeStruct((2 * rows, half), BF16),
        compiler_params=pltpu.CompilerParams(vmem_limit_bytes=40 * 2**20),
        name="normalise",
    )(core, keep, got, parts, gamma.reshape(1, half), beta.reshape(1, half))


def local(
    features, send_rows, send_counts, tile_src, edge_codes, degrees, w_self, w_neigh, gamma, beta
):
    rows, half = features.shape
    peers = lax.axis_size("dom")
    slots = send_rows.shape[2]
    tiles = rows // TILE // 2
    core = lax.axis_index("feat").astype(jnp.int32)
    core_arg = core.reshape(1)
    swap = [(0, 1), (1, 0)]

    other = lax.ppermute(features, "feat", swap)
    part = lax.dynamic_slice_in_dim(send_rows[0], core * (slots // 2), slots // 2, 1)
    slot_ids = jnp.arange(slots // 2, dtype=jnp.int32) + core * (slots // 2)
    idx = jnp.where(slot_ids[None, :] < send_counts[0][:, None], part, -1)
    idx = idx.reshape(peers // PEERS_STEP, PEERS_STEP, slots // 2).transpose(0, 2, 1)
    outgoing = pick_rows(idx, features, other)
    mine = lax.all_to_all(outgoing, "dom", split_axis=0, concat_axis=0, tiled=True)
    adj = adjacency(core_arg, edge_codes, tiles)
    sibling = lax.ppermute(mine, "feat", swap)

    def turned(w):
        return jnp.where(core == 0, w, jnp.roll(w, (half, half), (0, 1)))

    weights = jnp.concatenate([turned(w_self), turned(w_neigh)], axis=0)
    keep, send = aggregate(
        core_arg,
        tile_src,
        adj,
        degrees.reshape(-1, 1, TILE),
        weights,
        features,
        other,
        mine,
        sibling,
    )
    got = lax.ppermute(send, "feat", swap)
    parts = lax.all_to_all(
        moments(keep, got, peers), "dom", split_axis=0, concat_axis=0, tiled=True
    )
    return normalise(core_arg, keep, got, parts, gamma, beta)


def solution(mesh):
    return jax.shard_map(
        local,
        mesh=mesh,
        in_specs=(
            P("dom", "feat"),
            P("dom", None, None),
            P("dom", None),
            P("dom", None),
            P("dom", None, None),
            P("dom"),
            P(),
            P(),
            P("feat"),
            P("feat"),
        ),
        out_specs=P("dom", "feat"),
        check_vma=False,
    )
```

```python
import jax
import jax.numpy as jnp
from jax import lax
from jax.experimental import pallas as pl
from jax.experimental.pallas import tpu as pltpu
from jax.sharding import PartitionSpec as P

TILE = 128
PEERS_STEP = 8
EPS = 1e-05
BF16 = jnp.bfloat16
F32 = jnp.float32


def params(mib, axes=1):
    return pltpu.CompilerParams(
        dimension_semantics=("arbitrary",) * axes, vmem_limit_bytes=mib * 2**20
    )


def pick_kernel(idx_ref, own_ref, other_ref, out_ref, table):
    half = own_ref.shape[1]
    chunks = own_ref.shape[0] // TILE

    @pl.when(pl.program_id(0) == 0)
    def _():
        table[:, :half] = own_ref[...]
        table[:, half:] = other_ref[...]

    slots, peers = idx_ref.shape[1:]
    cols = idx_ref[0]
    lane = lax.broadcasted_iota(jnp.int32, (slots, TILE), 1)
    rows = []
    for p in range(peers):
        col = jnp.broadcast_to(cols[:, p : p + 1], (slots, TILE))
        low = jnp.where((col & (TILE - 1)) == lane, 1.0, 0.0).astype(BF16)
        high = (col >> 7).astype(F32).astype(BF16)
        zero = jnp.zeros_like(low)
        rows.append(
            jnp.concatenate(
                [jnp.where(high == jnp.asarray(c, BF16), low, zero) for c in range(chunks)],
                axis=1,
            )
        )
    hot = jnp.concatenate(rows, axis=0)
    picked = jnp.dot(hot, table[...], preferred_element_type=F32).astype(BF16)
    picked = picked.reshape(peers, slots, 2 * half)
    out_ref[:, :slots, :] = picked[:, :, :half]
    out_ref[:, slots:, :] = picked[:, :, half:]


def pick_rows(idx, own, other):
    groups, slots, peers = idx.shape
    rows, half = own.shape
    return pl.pallas_call(
        pick_kernel,
        grid=(groups,),
        in_specs=[
            pl.BlockSpec((1, slots, peers), lambda g: (g, 0, 0)),
            pl.BlockSpec((rows, half), lambda g: (0, 0)),
            pl.BlockSpec((rows, half), lambda g: (0, 0)),
        ],
        out_specs=pl.BlockSpec((peers, 2 * slots, half), lambda g: (g, 0, 0)),
        out_shape=pltpu.HBM((groups * peers, 2 * slots, half), BF16),
        scratch_shapes=[pltpu.VMEM((rows, 2 * half), BF16)],
        compiler_params=params(40),
        name="pick_rows",
    )(idx, own, other)


def adjacency_kernel(core_ref, codes_ref, out_ref):
    per_tile, edges = codes_ref.shape[1:]
    ids = lax.broadcasted_iota(jnp.int32, (TILE, edges), 0).astype(F32).astype(BF16)
    one = jnp.ones((TILE, edges), BF16)
    zero = jnp.zeros((TILE, edges), BF16)

    def hot(values):
        spread = jnp.broadcast_to(values.astype(F32), (16, edges)).astype(BF16)
        spread = jnp.concatenate([spread] * (TILE // 16), axis=0)
        return jnp.where(spread == ids, one, zero)

    for k in range(per_tile):
        codes = codes_ref[0, k : k + 1, :]
        counts = lax.dot_general(
            hot(codes >> 7),
            hot(codes & (TILE - 1)),
            (((1,), (1,)), ((), ())),
            preferred_element_type=F32,
        )
        out_ref[0, :, k * TILE : (k + 1) * TILE] = counts.astype(BF16)


def adjacency(core, codes, tiles):
    _, per_tile, edges = codes.shape
    return pl.pallas_call(
        adjacency_kernel,
        grid_spec=pltpu.PrefetchScalarGridSpec(
            num_scalar_prefetch=1,
            grid=(tiles,),
            in_specs=[
                pl.BlockSpec(
                    (1, per_tile, edges), lambda t, core_ref: (core_ref[0] * tiles + t, 0, 0)
                )
            ],
            out_specs=pl.BlockSpec((1, TILE, per_tile * TILE), lambda t, core_ref: (t, 0, 0)),
        ),
        out_shape=jax.ShapeDtypeStruct((tiles, TILE, per_tile * TILE), BF16),
        compiler_params=params(40),
        cost_estimate=pl.CostEstimate(
            flops=2 * tiles * per_tile * TILE * TILE * edges * 2,
            transcendentals=0,
            bytes_accessed=tiles * per_tile * (TILE * TILE * 2 + edges * 4),
        ),
        name="adjacency",
    )(core, codes)


def aggregate_kernel(
    core_ref,
    tile_src_ref,
    adj_ref,
    deg_ref,
    weight_ref,
    own_ref,
    other_ref,
    mine_ref,
    sibling_ref,
    keep_ref,
    send_ref,
    sources,
    sems,
):
    tiles, per_tile = tile_src_ref.shape
    tiles //= 2
    step = pl.program_id(0)
    core = core_ref[0]
    own_tiles = own_ref.shape[0]
    peers, slots, half = mine_ref.shape
    slots //= 2
    width = 2 * half
    lo = pl.ds(0, half)
    hi = pl.ds(half, half)

    @pl.when(step == 0)
    def _():
        owned = pl.ds(0, own_tiles)
        halo = pl.ds(own_tiles, peers)
        first = pl.ds(0, slots)
        second = pl.ds(slots, slots)
        here = pl.ds(pl.multiple_of(core * slots, slots), slots)
        there = pl.ds(pl.multiple_of((1 - core) * slots, slots), slots)
        copies = [
            pltpu.make_async_copy(own_ref, sources.at[owned, :, lo], sems.at[0]),
            pltpu.make_async_copy(other_ref, sources.at[owned, :, hi], sems.at[1]),
            pltpu.make_async_copy(
                mine_ref.at[:, first, :], sources.at[halo, here, lo], sems.at[2]
            ),
            pltpu.make_async_copy(
                mine_ref.at[:, second, :], sources.at[halo, here, hi], sems.at[3]
            ),
            pltpu.make_async_copy(
                sibling_ref.at[:, second, :], sources.at[halo, there, lo], sems.at[4]
            ),
            pltpu.make_async_copy(
                sibling_ref.at[:, first, :], sources.at[halo, there, hi], sems.at[5]
            ),
        ]
        for copy in copies:
            copy.start()
        for copy in copies:
            copy.wait()

    row = core * tiles + step
    total = jnp.zeros((TILE, width), F32)
    for k in range(0, per_tile, 2):
        pair = jnp.concatenate(
            [sources[tile_src_ref[row, k]], sources[tile_src_ref[row, k + 1]]], axis=0
        )
        total += jnp.dot(
            adj_ref[0, :, k * TILE : (k + 2) * TILE], pair, preferred_element_type=F32
        )
    degree = deg_ref[0].astype(F32)
    column = jnp.broadcast_to(degree, (8, TILE)).T[:, :1]
    mean_rows = (total / column).astype(BF16)
    both = jnp.concatenate([sources[row], mean_rows], axis=1)
    pre = jnp.dot(both, weight_ref[...], preferred_element_type=F32)
    keep_ref[...] = pre[:, :half]
    send_ref[...] = pre[:, half:]


def aggregate(core, tile_src, adj, degrees, weights, own, other, mine, sibling):
    tiles = adj.shape[0]
    half = mine.shape[2]
    width = 2 * half
    rows = tiles * TILE
    source_tiles = own.shape[0] // TILE + mine.shape[0]
    own = own.reshape(-1, TILE, half)
    other = other.reshape(-1, TILE, half)
    anywhere = pl.BlockSpec(memory_space=pl.ANY)
    return pl.pallas_call(
        aggregate_kernel,
        grid_spec=pltpu.PrefetchScalarGridSpec(
            num_scalar_prefetch=2,
            grid=(tiles,),
            in_specs=[
                pl.BlockSpec((1,) + adj.shape[1:], lambda t, c, s: (t, 0, 0)),
                pl.BlockSpec((1, 1, TILE), lambda t, c, s: (c[0] * tiles + t, 0, 0)),
                pl.BlockSpec(weights.shape, lambda t, c, s: (0, 0)),
                anywhere,
                anywhere,
                anywhere,
                anywhere,
            ],
            out_specs=[pl.BlockSpec((TILE, half), lambda t, c, s: (t, 0))] * 2,
            scratch_shapes=[
                pltpu.VMEM((source_tiles, TILE, width), BF16),
                pltpu.SemaphoreType.DMA((6,)),
            ],
        ),
        out_shape=[jax.ShapeDtypeStruct((rows, half), F32)] * 2,
        compiler_params=params(40),
        name="aggregate",
    )(core, tile_src, adj, degrees, weights, own, other, mine, sibling)


def moments_kernel(keep_ref, got_ref, out_ref):
    count = keep_ref.shape[0] + got_ref.shape[0]
    keep = keep_ref[...]
    got = got_ref[...]
    total = jnp.sum(keep, axis=0, keepdims=True) + jnp.sum(got, axis=0, keepdims=True)
    mean = total / count
    spread = jnp.sum(jnp.square(keep - mean), axis=0, keepdims=True) + jnp.sum(
        jnp.square(got - mean), axis=0, keepdims=True
    )
    both = jnp.concatenate([total, spread], axis=0)
    out_ref[...] = jnp.broadcast_to(both[None], out_ref.shape)


def moments(keep, got, peers):
    return pl.pallas_call(
        moments_kernel,
        out_shape=jax.ShapeDtypeStruct((peers, 2, keep.shape[1]), F32),
        compiler_params=pltpu.CompilerParams(vmem_limit_bytes=40 * 2**20),
        name="moments",
    )(keep, got)


def normalise_kernel(core_ref, keep_ref, got_ref, parts_ref, gamma_ref, beta_ref, out_ref):
    rows = keep_ref.shape[0]
    count = float(2 * rows)
    parts = parts_ref[...]
    peers = parts.shape[0]
    totals = parts[:, 0, :]
    spreads = parts[:, 1, :]
    mean = jnp.sum(totals, axis=0, keepdims=True) / (count * peers)
    shift = totals / count - mean
    var = jnp.sum(spreads + count * shift * shift, axis=0, keepdims=True) / (count * peers)
    scale = gamma_ref[...] / jnp.sqrt(var + EPS)
    beta = beta_ref[...]
    here = pl.multiple_of(core_ref[0] * rows, rows)
    there = pl.multiple_of((1 - core_ref[0]) * rows, rows)
    out_ref[pl.ds(here, rows), :] = jnp.maximum(
        (keep_ref[...] - mean) * scale + beta, 0.0
    ).astype(BF16)
    out_ref[pl.ds(there, rows), :] = jnp.maximum(
        (got_ref[...] - mean) * scale + beta, 0.0
    ).astype(BF16)


def normalise(core, keep, got, parts, gamma, beta):
    rows, half = keep.shape
    whole = pl.BlockSpec(memory_space=pltpu.VMEM)
    return pl.pallas_call(
        normalise_kernel,
        in_specs=[pl.BlockSpec(memory_space=pltpu.SMEM)] + [whole] * 5,
        out_specs=whole,
        out_shape=jax.ShapeDtypeStruct((2 * rows, half), BF16),
        compiler_params=pltpu.CompilerParams(vmem_limit_bytes=40 * 2**20),
        name="normalise",
    )(core, keep, got, parts, gamma.reshape(1, half), beta.reshape(1, half))


def local(
    features, send_rows, send_counts, tile_src, edge_codes, degrees, w_self, w_neigh, gamma, beta
):
    rows, half = features.shape
    peers = lax.axis_size("dom")
    slots = send_rows.shape[2]
    tiles = rows // TILE // 2
    core = lax.axis_index("feat").astype(jnp.int32)
    core_arg = core.reshape(1)
    swap = [(0, 1), (1, 0)]

    other = lax.ppermute(features, "feat", swap)
    part = lax.dynamic_slice_in_dim(send_rows[0], core * (slots // 2), slots // 2, 1)
    slot_ids = jnp.arange(slots // 2, dtype=jnp.int32) + core * (slots // 2)
    idx = jnp.where(slot_ids[None, :] < send_counts[0][:, None], part, -1)
    idx = idx.reshape(peers // PEERS_STEP, PEERS_STEP, slots // 2).transpose(0, 2, 1)
    outgoing = pick_rows(idx, features, other)
    mine = lax.all_to_all(outgoing, "dom", split_axis=0, concat_axis=0, tiled=True)
    adj = adjacency(core_arg, edge_codes, tiles)
    mine, adj = lax.optimization_barrier((mine, adj))
    sibling = lax.ppermute(mine, "feat", swap)

    def turned(w):
        return jnp.where(core == 0, w, jnp.roll(w, (half, half), (0, 1)))

    weights = jnp.concatenate([turned(w_self), turned(w_neigh)], axis=0)
    keep, send = aggregate(
        core_arg,
        tile_src,
        adj,
        degrees.reshape(-1, 1, TILE),
        weights,
        features,
        other,
        mine,
        sibling,
    )
    got = lax.ppermute(send, "feat", swap)
    parts = lax.all_to_all(
        moments(keep, got, peers), "dom", split_axis=0, concat_axis=0, tiled=True
    )
    return normalise(core_arg, keep, got, parts, gamma, beta)


def solution(mesh):
    return jax.shard_map(
        local,
        mesh=mesh,
        in_specs=(
            P("dom", "feat"),
            P("dom", None, None),
            P("dom", None),
            P("dom", None),
            P("dom", None, None),
            P("dom"),
            P(),
            P(),
            P("feat"),
            P("feat"),
        ),
        out_specs=P("dom", "feat"),
        check_vma=False,
    )
```

```python
import jax
import jax.numpy as jnp
from jax import lax
from jax.experimental import pallas as pl
from jax.experimental.pallas import tpu as pltpu
from jax.sharding import PartitionSpec as P

TILE = 128
PEERS_STEP = 8
TILES_STEP = 4
LOAD_PARTS = 4
EPS = 1e-05
BF16 = jnp.bfloat16
F32 = jnp.float32
F8 = jnp.float8_e4m3fn


def params(mib, axes=1):
    return pltpu.CompilerParams(
        dimension_semantics=("arbitrary",) * axes, vmem_limit_bytes=mib * 2**20
    )


def in_hbm(array):
    return pltpu.with_memory_space_constraint(array, pltpu.HBM)


def pick_kernel(rows_ref, counts_ref, own_ref, out_ref, rows, counts, loaded, table, lines, sems):
    step = pl.program_id(0)
    peers, slots, half = out_ref.shape

    @pl.when(step == 0)
    def _():
        part = own_ref.shape[0] // LOAD_PARTS
        copies = [
            pltpu.make_async_copy(
                own_ref.at[pl.ds(q * part, part)], loaded.at[pl.ds(q * part, part)], sems.at[q]
            )
            for q in range(LOAD_PARTS)
        ]
        row_copy = pltpu.make_async_copy(rows_ref, rows, sems.at[LOAD_PARTS])
        count_copy = pltpu.make_async_copy(counts_ref, counts, sems.at[LOAD_PARTS + 1])
        for copy in copies:
            copy.start()
        row_copy.start()
        count_copy.start()
        for q, copy in enumerate(copies):
            copy.wait()
            table[q * part : (q + 1) * part, :] = loaded[q * part : (q + 1) * part, :].astype(F32)
        row_copy.wait()
        count_copy.wait()

    for p in range(peers):
        for s in range(slots):
            at = p * slots + s
            lines[at : at + 1, :] = table[pl.ds(rows[0, step * peers + p, s], 1), :]
    slot = lax.broadcasted_iota(jnp.int32, (slots, half), 0)
    for p in range(peers):
        live = slot < counts[0, step * peers + p]
        block = lines[p * slots : (p + 1) * slots, :]
        out_ref[p] = jnp.where(live, block, 0.0).astype(BF16)


def pick_rows(send_rows, send_counts, own):
    _, peers, slots = send_rows.shape
    rows, half = own.shape
    hbm = pl.BlockSpec(memory_space=pltpu.HBM)
    return pl.pallas_call(
        pick_kernel,
        grid=(peers // PEERS_STEP,),
        in_specs=[hbm, hbm, hbm],
        out_specs=pl.BlockSpec((PEERS_STEP, slots, half), lambda g: (g, 0, 0)),
        out_shape=pltpu.HBM((peers, slots, half), BF16),
        scratch_shapes=[
            pltpu.SMEM(send_rows.shape, jnp.int32),
            pltpu.SMEM(send_counts.shape, jnp.int32),
            pltpu.VMEM((rows, half), BF16),
            pltpu.VMEM((rows, half), F32),
            pltpu.VMEM((PEERS_STEP * slots, half), F32),
            pltpu.SemaphoreType.DMA((LOAD_PARTS + 2,)),
        ],
        compiler_params=params(16),
        name="pick_rows",
    )(in_hbm(send_rows), in_hbm(send_counts), in_hbm(own))


def adjacency_kernel(core_ref, codes_ref, out_ref):
    per_tile, edges = codes_ref.shape[1:]
    ids = lax.broadcasted_iota(jnp.int32, (TILE, edges), 0).astype(F32).astype(BF16)
    one = jnp.ones((TILE, edges), BF16)
    zero = jnp.zeros((TILE, edges), BF16)

    def hot(values):
        spread = jnp.broadcast_to(values.astype(F32), (16, edges)).astype(BF16)
        spread = jnp.concatenate([spread] * (TILE // 16), axis=0)
        return jnp.where(spread == ids, one, zero).astype(F8)

    for k in range(per_tile):
        codes = codes_ref[0, k : k + 1, :]
        counts = lax.dot_general(
            hot(codes >> 7),
            hot(codes & (TILE - 1)),
            (((1,), (1,)), ((), ())),
            preferred_element_type=F32,
        )
        out_ref[0, :, k * TILE : (k + 1) * TILE] = counts.astype(BF16)


def adjacency(core, codes, tiles):
    _, per_tile, edges = codes.shape
    return pl.pallas_call(
        adjacency_kernel,
        grid_spec=pltpu.PrefetchScalarGridSpec(
            num_scalar_prefetch=1,
            grid=(tiles,),
            in_specs=[
                pl.BlockSpec(
                    (1, per_tile, edges), lambda t, core_ref: (core_ref[0] * tiles + t, 0, 0)
                )
            ],
            out_specs=pl.BlockSpec((1, TILE, per_tile * TILE), lambda t, core_ref: (t, 0, 0)),
        ),
        out_shape=pltpu.HBM((tiles, TILE, per_tile * TILE), BF16),
        compiler_params=params(16),
        cost_estimate=pl.CostEstimate(
            flops=2 * tiles * per_tile * TILE * TILE * edges * 2,
            transcendentals=0,
            bytes_accessed=tiles * per_tile * (TILE * TILE * 2 + edges * 4),
        ),
        name="adjacency",
    )(core, in_hbm(codes))


def aggregate_kernel(
    core_ref,
    tile_src_ref,
    adj_ref,
    deg_ref,
    weight_ref,
    own_ref,
    other_ref,
    mine_ref,
    sibling_ref,
    keep_ref,
    send_ref,
    keep_stats_ref,
    send_stats_ref,
    near,
    far,
    sems,
):
    per_tile = tile_src_ref.shape[1]
    step = pl.program_id(0)
    steps = pl.num_programs(0)
    core = core_ref[0]
    own_tiles, _, half = own_ref.shape
    peers = mine_ref.shape[0]

    @pl.when(step == 0)
    def _():
        owned = pl.ds(0, own_tiles)
        halo = pl.ds(own_tiles, peers)
        copies = [
            pltpu.make_async_copy(own_ref, near.at[owned], sems.at[0]),
            pltpu.make_async_copy(other_ref, far.at[owned], sems.at[1]),
            pltpu.make_async_copy(mine_ref, near.at[halo], sems.at[2]),
            pltpu.make_async_copy(sibling_ref, far.at[halo], sems.at[3]),
        ]
        for copy in copies:
            copy.start()
        for copy in copies:
            copy.wait()

    def source(number):
        return jnp.concatenate([near[number], far[number]], axis=1)

    first = core * (own_tiles // 2) + step * TILES_STEP
    inputs = []
    for q in range(TILES_STEP):
        row = first + q
        total = jnp.zeros((TILE, 2 * half), F32)
        for k in range(0, per_tile, 2):
            pair = jnp.concatenate(
                [source(tile_src_ref[row, k]), source(tile_src_ref[row, k + 1])], axis=0
            )
            total += jnp.dot(
                adj_ref[q, :, k * TILE : (k + 2) * TILE], pair, preferred_element_type=F32
            )
        degree = jnp.broadcast_to(deg_ref[q].astype(F32), (8, TILE)).T[:, :1]
        inputs.append(jnp.concatenate([source(row), (total / degree).astype(BF16)], axis=1))
    pre = jnp.dot(
        jnp.concatenate(inputs, axis=0), weight_ref[...], preferred_element_type=F32
    )
    rows = TILES_STEP * TILE
    here = pl.ds(pl.multiple_of(step * rows, rows), rows)
    keep_ref[here, :] = pre[:, :half]
    send_ref[here, :] = pre[:, half:]

    @pl.when(step == steps - 1)
    def _():
        for values_ref, stats_ref in ((keep_ref, keep_stats_ref), (send_ref, send_stats_ref)):
            values = values_ref[...]
            sums = jnp.sum(values, axis=0, keepdims=True)
            centred = values - sums / values.shape[0]
            stats_ref[0:1, :] = sums
            stats_ref[1:2, :] = jnp.sum(centred * centred, axis=0, keepdims=True)


def aggregate(core, tile_src, adj, degrees, weights, own, other, mine, sibling):
    tiles = adj.shape[0]
    half = mine.shape[2]
    rows = tiles * TILE
    steps = tiles // TILES_STEP
    own = own.reshape(-1, TILE, half)
    other = other.reshape(-1, TILE, half)
    source_tiles = own.shape[0] + mine.shape[0]
    anywhere = pl.BlockSpec(memory_space=pl.ANY)
    vmem = pl.BlockSpec(memory_space=pltpu.VMEM)
    return pl.pallas_call(
        aggregate_kernel,
        grid_spec=pltpu.PrefetchScalarGridSpec(
            num_scalar_prefetch=2,
            grid=(steps,),
            in_specs=[
                pl.BlockSpec((TILES_STEP,) + adj.shape[1:], lambda t, c, s: (t, 0, 0)),
                pl.BlockSpec((TILES_STEP, 1, TILE), lambda t, c, s: (c[0] * steps + t, 0, 0)),
                vmem,
                anywhere,
                anywhere,
                anywhere,
                anywhere,
            ],
            out_specs=[vmem] * 4,
            scratch_shapes=[
                pltpu.VMEM((source_tiles, TILE, half), BF16),
                pltpu.VMEM((source_tiles, TILE, half), BF16),
                pltpu.SemaphoreType.DMA((4,)),
            ],
        ),
        out_shape=[jax.ShapeDtypeStruct((rows, half), F32)] * 2
        + [jax.ShapeDtypeStruct((2, half), F32)] * 2,
        compiler_params=params(32),
        name="aggregate",
    )(core, tile_src, in_hbm(adj), degrees, weights, own, other, mine, sibling)


def normalise_kernel(core_ref, keep_ref, got_ref, parts_ref, gamma_ref, beta_ref, out_ref):
    rows = keep_ref.shape[0]
    parts = parts_ref[...]
    members = 2.0 * parts.shape[0]
    sums = jnp.concatenate([parts[:, 0, :], parts[:, 2, :]], axis=0)
    spreads = jnp.concatenate([parts[:, 1, :], parts[:, 3, :]], axis=0)
    mean = jnp.sum(sums, axis=0, keepdims=True) / (rows * members)
    shift = sums / rows - mean
    var = jnp.sum(spreads + rows * (shift * shift), axis=0, keepdims=True) / (rows * members)
    scale = gamma_ref[...] / jnp.sqrt(var + EPS)
    beta = beta_ref[...]
    here = pl.multiple_of(core_ref[0] * rows, rows)
    there = pl.multiple_of((1 - core_ref[0]) * rows, rows)
    out_ref[pl.ds(here, rows), :] = jnp.maximum(
        (keep_ref[...] - mean) * scale + beta, 0.0
    ).astype(BF16)
    out_ref[pl.ds(there, rows), :] = jnp.maximum(
        (got_ref[...] - mean) * scale + beta, 0.0
    ).astype(BF16)


def normalise(core, keep, got, parts, gamma, beta):
    rows, half = keep.shape
    whole = pl.BlockSpec(memory_space=pltpu.VMEM)
    return pl.pallas_call(
        normalise_kernel,
        in_specs=[pl.BlockSpec(memory_space=pltpu.SMEM)] + [whole] * 5,
        out_specs=whole,
        out_shape=jax.ShapeDtypeStruct((2 * rows, half), BF16),
        compiler_params=pltpu.CompilerParams(vmem_limit_bytes=32 * 2**20),
        name="normalise",
    )(core, keep, got, parts, gamma.reshape(1, half), beta.reshape(1, half))


def local(
    features, send_rows, send_counts, tile_src, edge_codes, degrees, w_self, w_neigh, gamma, beta
):
    rows, half = features.shape
    peers = lax.axis_size("dom")
    tiles = rows // TILE // 2
    core = lax.axis_index("feat").astype(jnp.int32)
    core_arg = core.reshape(1)
    swap = [(0, 1), (1, 0)]

    outgoing = pick_rows(send_rows, send_counts, features)
    mine = lax.all_to_all(outgoing, "dom", split_axis=0, concat_axis=0, tiled=True)
    other = lax.ppermute(features, "feat", swap)
    adj = adjacency(core_arg, edge_codes, tiles)

    def turned(w):
        return jnp.where(core == 0, w, jnp.roll(w, (half, half), (0, 1)))

    weights = jnp.concatenate([turned(w_self), turned(w_neigh)], axis=0)
    mine, adj, other, weights = lax.optimization_barrier((mine, adj, other, weights))
    sibling = lax.ppermute(mine, "feat", swap)
    keep, send, keep_stats, send_stats = aggregate(
        core_arg,
        tile_src,
        adj,
        degrees.reshape(-1, 1, TILE),
        weights,
        features,
        other,
        mine,
        sibling,
    )
    got_stats = lax.ppermute(send_stats, "feat", swap)
    got = lax.ppermute(send, "feat", swap)
    stats = jnp.concatenate([keep_stats, got_stats], axis=0)
    stats = jnp.broadcast_to(stats[None], (peers,) + stats.shape)
    parts = lax.all_to_all(stats, "dom", split_axis=0, concat_axis=0, tiled=True)
    return normalise(core_arg, keep, got, parts, gamma, beta)


def solution(mesh):
    return jax.shard_map(
        local,
        mesh=mesh,
        in_specs=(
            P("dom", "feat"),
            P("dom", None, None),
            P("dom", None),
            P("dom", None),
            P("dom", None, None),
            P("dom"),
            P(),
            P(),
            P("feat"),
            P("feat"),
        ),
        out_specs=P("dom", "feat"),
        check_vma=False,
    )
```

```python
import jax
import jax.numpy as jnp
from jax import lax
from jax.experimental import pallas as pl
from jax.experimental.pallas import tpu as pltpu
from jax.sharding import PartitionSpec as P

TILE = 128
PEERS_STEP = 4
TILES_STEP = 4
PAIR = 2
LOAD_PARTS = 4
EPS = 1e-05
BF16 = jnp.bfloat16
F32 = jnp.float32
F8 = jnp.float8_e4m3fn


def params(mib, axes=1):
    return pltpu.CompilerParams(
        dimension_semantics=("arbitrary",) * axes, vmem_limit_bytes=mib * 2**20
    )


def in_hbm(array):
    return pltpu.with_memory_space_constraint(array, pltpu.HBM)


def pick_kernel(rows_ref, counts_ref, own_ref, out_ref, rows, counts, loaded, table, lines, sems):
    peers, slots, half = out_ref.shape
    part = own_ref.shape[0] // LOAD_PARTS
    row_copy = pltpu.make_async_copy(rows_ref, rows, sems.at[LOAD_PARTS])
    count_copy = pltpu.make_async_copy(counts_ref, counts, sems.at[LOAD_PARTS + 1])
    copies = [
        pltpu.make_async_copy(
            own_ref.at[pl.ds(q * part, part)], loaded.at[pl.ds(q * part, part)], sems.at[q]
        )
        for q in range(LOAD_PARTS)
    ]
    row_copy.start()
    count_copy.start()
    for copy in copies:
        copy.start()
    for q, copy in enumerate(copies):
        copy.wait()
        table[q * part : (q + 1) * part, :] = loaded[q * part : (q + 1) * part, :].astype(F32)
    row_copy.wait()
    count_copy.wait()
    slot = lax.broadcasted_iota(jnp.int32, (slots, half), 0)

    def group(g, carry):
        for p in range(PEERS_STEP):
            for s in range(slots):
                at = p * slots + s
                lines[at : at + 1, :] = table[pl.ds(rows[0, g * PEERS_STEP + p, s], 1), :]
        for p in range(PEERS_STEP):
            peer = g * PEERS_STEP + p
            block = lines[p * slots : (p + 1) * slots, :]
            out_ref[peer] = jnp.where(slot < counts[0, peer], block, 0.0).astype(BF16)
        return carry

    lax.fori_loop(0, peers // PEERS_STEP, group, 0)


def pick_rows(send_rows, send_counts, own):
    _, peers, slots = send_rows.shape
    rows, half = own.shape
    hbm = pl.BlockSpec(memory_space=pltpu.HBM)
    return pl.pallas_call(
        pick_kernel,
        in_specs=[hbm, hbm, hbm],
        out_specs=pl.BlockSpec(memory_space=pltpu.VMEM),
        out_shape=jax.ShapeDtypeStruct((peers, slots, half), BF16),
        scratch_shapes=[
            pltpu.SMEM(send_rows.shape, jnp.int32),
            pltpu.SMEM(send_counts.shape, jnp.int32),
            pltpu.VMEM((rows, half), BF16),
            pltpu.VMEM((rows, half), F32),
            pltpu.VMEM((PEERS_STEP * slots, half), F32),
            pltpu.SemaphoreType.DMA((LOAD_PARTS + 2,)),
        ],
        compiler_params=pltpu.CompilerParams(vmem_limit_bytes=10 * 2**20),
        name="pick_rows",
    )(in_hbm(send_rows), in_hbm(send_counts), in_hbm(own))


def adjacency_kernel(core_ref, codes_ref, out_ref):
    per_tile, edges = codes_ref.shape[1:]
    ids = lax.broadcasted_iota(jnp.int32, (TILE, edges), 0).astype(F32).astype(BF16)
    one = jnp.ones((TILE, edges), BF16)
    zero = jnp.zeros((TILE, edges), BF16)

    def hot(values):
        spread = jnp.broadcast_to(values.astype(F32), (16, edges)).astype(BF16)
        spread = jnp.concatenate([spread] * (TILE // 16), axis=0)
        return jnp.where(spread == ids, one, zero).astype(F8)

    for q in range(PAIR):
        for k in range(per_tile):
            codes = codes_ref[q, k : k + 1, :]
            counts = lax.dot_general(
                hot(codes >> 7),
                hot(codes & (TILE - 1)),
                (((1,), (1,)), ((), ())),
                preferred_element_type=F32,
            )
            out_ref[q, :, k * TILE : (k + 1) * TILE] = counts.astype(BF16)


def adjacency(core, codes, tiles):
    _, per_tile, edges = codes.shape
    steps = tiles // PAIR
    return pl.pallas_call(
        adjacency_kernel,
        grid_spec=pltpu.PrefetchScalarGridSpec(
            num_scalar_prefetch=1,
            grid=(steps,),
            in_specs=[
                pl.BlockSpec(
                    (PAIR, per_tile, edges), lambda t, core_ref: (core_ref[0] * steps + t, 0, 0)
                )
            ],
            out_specs=pl.BlockSpec((PAIR, TILE, per_tile * TILE), lambda t, core_ref: (t, 0, 0)),
        ),
        out_shape=pltpu.HBM((tiles, TILE, per_tile * TILE), BF16),
        compiler_params=params(12),
        cost_estimate=pl.CostEstimate(
            flops=2 * tiles * per_tile * TILE * TILE * edges * 2,
            transcendentals=0,
            bytes_accessed=tiles * per_tile * (TILE * TILE * 2 + edges * 4),
        ),
        name="adjacency",
    )(core, in_hbm(codes))


def stage_kernel(own_ref, mine_ref, adj_ref, near_ref, early_ref, sems):
    own_tiles = own_ref.shape[0]
    copies = [
        pltpu.make_async_copy(own_ref, near_ref.at[pl.ds(0, own_tiles)], sems.at[0]),
        pltpu.make_async_copy(
            mine_ref, near_ref.at[pl.ds(own_tiles, mine_ref.shape[0])], sems.at[1]
        ),
    ]
    for t in range(early_ref.shape[0]):
        copies.append(pltpu.make_async_copy(adj_ref.at[t], early_ref.at[t], sems.at[2 + t]))
    for copy in copies:
        copy.start()
    for copy in copies:
        copy.wait()


def stage(own, mine, adj):
    early = adj.shape[0] // 2
    source_tiles = own.shape[0] + mine.shape[0]
    return pl.pallas_call(
        stage_kernel,
        in_specs=[
            pl.BlockSpec(memory_space=pl.ANY),
            pl.BlockSpec(memory_space=pl.ANY),
            pl.BlockSpec(memory_space=pltpu.HBM),
        ],
        out_specs=[pl.BlockSpec(memory_space=pltpu.VMEM)] * 2,
        out_shape=[
            jax.ShapeDtypeStruct((source_tiles,) + own.shape[1:], BF16),
            jax.ShapeDtypeStruct((early,) + adj.shape[1:], BF16),
        ],
        scratch_shapes=[pltpu.SemaphoreType.DMA((2 + early,))],
        compiler_params=pltpu.CompilerParams(vmem_limit_bytes=2 * 2**20),
        name="stage",
    )(own, mine, in_hbm(adj))


def aggregate_kernel(
    core_ref,
    tile_src_ref,
    adj_ref,
    deg_ref,
    weight_ref,
    other_ref,
    sibling_ref,
    near,
    early,
    keep_ref,
    send_ref,
    keep_stats_ref,
    send_stats_ref,
    far,
    late,
    sems,
):
    per_tile = tile_src_ref.shape[1]
    own_tiles, _, half = other_ref.shape
    peers = sibling_ref.shape[0]
    tiles = adj_ref.shape[0]
    ahead = early.shape[0]
    core = core_ref[0]

    def late_copy(t):
        return pltpu.make_async_copy(adj_ref.at[ahead + t], late.at[t], sems.at[2 + t])

    copies = [
        pltpu.make_async_copy(other_ref, far.at[pl.ds(0, own_tiles)], sems.at[0]),
        pltpu.make_async_copy(sibling_ref, far.at[pl.ds(own_tiles, peers)], sems.at[1]),
    ]
    for copy in copies:
        copy.start()
    for t in range(tiles - ahead):
        late_copy(t).start()
    for copy in copies:
        copy.wait()

    def source(number):
        return jnp.concatenate([near[number], far[number]], axis=1)

    def block(counts, base, at):
        inputs = []
        for q in range(TILES_STEP):
            row = core * tiles + base + at + q
            total = jnp.zeros((TILE, 2 * half), F32)
            for k in range(0, per_tile, 2):
                pair = jnp.concatenate(
                    [source(tile_src_ref[row, k]), source(tile_src_ref[row, k + 1])], axis=0
                )
                total += jnp.dot(
                    counts[at + q, :, k * TILE : (k + 2) * TILE],
                    pair,
                    preferred_element_type=F32,
                )
            degree = jnp.broadcast_to(deg_ref[row].astype(F32), (8, TILE)).T[:, :1]
            inputs.append(jnp.concatenate([source(row), (total / degree).astype(BF16)], axis=1))
        pre = jnp.dot(
            jnp.concatenate(inputs, axis=0), weight_ref[...], preferred_element_type=F32
        )
        rows = TILES_STEP * TILE
        here = pl.ds(pl.multiple_of((base + at) * TILE, rows), rows)
        keep_ref[here, :] = pre[:, :half]
        send_ref[here, :] = pre[:, half:]

    def early_step(step, carry):
        block(early, 0, step * TILES_STEP)
        return carry

    def late_step(step, carry):
        for q in range(TILES_STEP):
            late_copy(step * TILES_STEP + q).wait()
        block(late, ahead, step * TILES_STEP)
        return carry

    lax.fori_loop(0, ahead // TILES_STEP, early_step, 0)
    lax.fori_loop(0, (tiles - ahead) // TILES_STEP, late_step, 0)
    for values_ref, stats_ref in ((keep_ref, keep_stats_ref), (send_ref, send_stats_ref)):
        values = values_ref[...]
        sums = jnp.sum(values, axis=0, keepdims=True)
        centred = values - sums / values.shape[0]
        stats_ref[0:1, :] = sums
        stats_ref[1:2, :] = jnp.sum(centred * centred, axis=0, keepdims=True)


def aggregate(core, tile_src, adj, degrees, weights, other, sibling, near, early):
    tiles = adj.shape[0]
    late = tiles - early.shape[0]
    half = sibling.shape[2]
    rows = tiles * TILE
    smem = pl.BlockSpec(memory_space=pltpu.SMEM)
    vmem = pl.BlockSpec(memory_space=pltpu.VMEM)
    anywhere = pl.BlockSpec(memory_space=pl.ANY)
    hbm = pl.BlockSpec(memory_space=pltpu.HBM)
    return pl.pallas_call(
        aggregate_kernel,
        in_specs=[smem, smem, hbm, vmem, vmem, anywhere, anywhere, vmem, vmem],
        out_specs=[vmem] * 4,
        out_shape=[jax.ShapeDtypeStruct((rows, half), F32)] * 2
        + [jax.ShapeDtypeStruct((2, half), F32)] * 2,
        scratch_shapes=[
            pltpu.VMEM(near.shape, BF16),
            pltpu.VMEM((late,) + adj.shape[1:], BF16),
            pltpu.SemaphoreType.DMA((2 + late,)),
        ],
        compiler_params=pltpu.CompilerParams(vmem_limit_bytes=20 * 2**20),
        name="aggregate",
    )(core, tile_src, in_hbm(adj), degrees, weights, other, sibling, near, early)


def normalise_kernel(core_ref, keep_ref, got_ref, parts_ref, gamma_ref, beta_ref, out_ref):
    rows = keep_ref.shape[0]
    parts = parts_ref[...]
    members = 2.0 * parts.shape[0]
    sums = jnp.concatenate([parts[:, 0, :], parts[:, 2, :]], axis=0)
    spreads = jnp.concatenate([parts[:, 1, :], parts[:, 3, :]], axis=0)
    mean = jnp.sum(sums, axis=0, keepdims=True) / (rows * members)
    shift = sums / rows - mean
    var = jnp.sum(spreads + rows * (shift * shift), axis=0, keepdims=True) / (rows * members)
    scale = gamma_ref[...] / jnp.sqrt(var + EPS)
    beta = beta_ref[...]
    here = pl.multiple_of(core_ref[0] * rows, rows)
    there = pl.multiple_of((1 - core_ref[0]) * rows, rows)
    out_ref[pl.ds(here, rows), :] = jnp.maximum(
        (keep_ref[...] - mean) * scale + beta, 0.0
    ).astype(BF16)
    out_ref[pl.ds(there, rows), :] = jnp.maximum(
        (got_ref[...] - mean) * scale + beta, 0.0
    ).astype(BF16)


def normalise(core, keep, got, parts, gamma, beta):
    rows, half = keep.shape
    whole = pl.BlockSpec(memory_space=pltpu.VMEM)
    return pl.pallas_call(
        normalise_kernel,
        in_specs=[pl.BlockSpec(memory_space=pltpu.SMEM)] + [whole] * 5,
        out_specs=whole,
        out_shape=jax.ShapeDtypeStruct((2 * rows, half), BF16),
        compiler_params=pltpu.CompilerParams(vmem_limit_bytes=8 * 2**20),
        name="normalise",
    )(core, keep, got, parts, gamma.reshape(1, half), beta.reshape(1, half))


def local(
    features, send_rows, send_counts, tile_src, edge_codes, degrees, w_self, w_neigh, gamma, beta
):
    rows, half = features.shape
    peers = lax.axis_size("dom")
    tiles = rows // TILE // 2
    core = lax.axis_index("feat").astype(jnp.int32)
    core_arg = core.reshape(1)
    swap = [(0, 1), (1, 0)]

    outgoing = pick_rows(send_rows, send_counts, features)
    mine = lax.all_to_all(outgoing, "dom", split_axis=0, concat_axis=0, tiled=True)
    other = lax.ppermute(features, "feat", swap)
    adj = adjacency(core_arg, edge_codes, tiles)

    def turned(w):
        return jnp.where(core == 0, w, jnp.roll(w, (half, half), (0, 1)))

    weights = jnp.concatenate([turned(w_self), turned(w_neigh)], axis=0)
    mine, adj, other, weights = lax.optimization_barrier((mine, adj, other, weights))
    sibling = lax.ppermute(mine, "feat", swap)
    other = other.reshape(-1, TILE, half)
    near, early = stage(features.reshape(-1, TILE, half), mine, adj)
    keep, send, keep_stats, send_stats = aggregate(
        core_arg,
        tile_src,
        adj,
        degrees.reshape(-1, 1, TILE),
        weights,
        other,
        sibling,
        near,
        early,
    )
    got_stats = lax.ppermute(send_stats, "feat", swap)
    got = lax.ppermute(send, "feat", swap)
    stats = jnp.concatenate([keep_stats, got_stats], axis=0)
    stats = jnp.broadcast_to(stats[None], (peers,) + stats.shape)
    parts = lax.all_to_all(stats, "dom", split_axis=0, concat_axis=0, tiled=True)
    return normalise(core_arg, keep, got, parts, gamma, beta)


def solution(mesh):
    return jax.shard_map(
        local,
        mesh=mesh,
        in_specs=(
            P("dom", "feat"),
            P("dom", None, None),
            P("dom", None),
            P("dom", None),
            P("dom", None, None),
            P("dom"),
            P(),
            P(),
            P("feat"),
            P("feat"),
        ),
        out_specs=P("dom", "feat"),
        check_vma=False,
    )
```

```python
import jax
import jax.numpy as jnp
from jax import lax
from jax.experimental import pallas as pl
from jax.experimental.pallas import tpu as pltpu
from jax.sharding import PartitionSpec as P

TILE = 128
PEERS_STEP = 4
RING = 4
TILES_STEP = 4
PAIR = 2
LOAD_PARTS = 4
EPS = 1e-05
BF16 = jnp.bfloat16
F32 = jnp.float32
F8 = jnp.float8_e4m3fn


def params(mib, axes=1):
    return pltpu.CompilerParams(
        dimension_semantics=("arbitrary",) * axes, vmem_limit_bytes=mib * 2**20
    )


def in_hbm(array):
    return pltpu.with_memory_space_constraint(array, pltpu.HBM)


def pick_kernel(rows_ref, counts_ref, own_ref, out_ref, *scratch):
    ring = scratch[:RING]
    counts, loaded, table, lines, done, own_sems, ring_sems, count_sem, out_sems = scratch[RING:]
    peers, slots, half = out_ref.shape
    part = own_ref.shape[0] // LOAD_PARTS
    rounds = peers // (PEERS_STEP * RING)

    def row_copy(g, b):
        wanted = rows_ref.at[0, pl.ds(g * PEERS_STEP, PEERS_STEP)]
        return pltpu.make_async_copy(wanted, ring[b], ring_sems.at[b])

    def out_copy(g):
        at = pl.ds(g * PEERS_STEP, PEERS_STEP)
        return pltpu.make_async_copy(done.at[at], out_ref.at[at], out_sems.at[g])

    count_copy = pltpu.make_async_copy(counts_ref, counts, count_sem)
    own_copies = [
        pltpu.make_async_copy(
            own_ref.at[pl.ds(q * part, part)], loaded.at[pl.ds(q * part, part)], own_sems.at[q]
        )
        for q in range(LOAD_PARTS)
    ]
    for b in range(RING):
        row_copy(b, b).start()
    count_copy.start()
    for copy in own_copies:
        copy.start()
    for q, copy in enumerate(own_copies):
        copy.wait()
        table[q * part : (q + 1) * part, :] = loaded[q * part : (q + 1) * part, :].astype(F32)
    count_copy.wait()
    slot = lax.broadcasted_iota(jnp.int32, (slots, half), 0)

    def one_round(i, carry):
        for b in range(RING):
            g = i * RING + b
            row_copy(g, b).wait()
            for p in range(PEERS_STEP):
                for s in range(slots):
                    at = p * slots + s
                    lines[at : at + 1, :] = table[pl.ds(ring[b][p, s], 1), :]

            @pl.when(i < rounds - 1)
            def _():
                row_copy(g + RING, b).start()

            for p in range(PEERS_STEP):
                peer = g * PEERS_STEP + p
                block = lines[p * slots : (p + 1) * slots, :]
                done[peer] = jnp.where(slot < counts[0, peer], block, 0.0).astype(BF16)
            out_copy(g).start()
        return carry

    def finish(g, carry):
        out_copy(g).wait()
        return carry

    lax.fori_loop(0, rounds, one_round, 0)
    lax.fori_loop(0, peers // PEERS_STEP, finish, 0)


def pick_rows(send_rows, send_counts, own):
    _, peers, slots = send_rows.shape
    rows, half = own.shape
    hbm = pl.BlockSpec(memory_space=pltpu.HBM)
    return pl.pallas_call(
        pick_kernel,
        in_specs=[hbm, hbm, hbm],
        out_specs=hbm,
        out_shape=pltpu.HBM((peers, slots, half), BF16),
        scratch_shapes=[pltpu.SMEM((PEERS_STEP, slots), jnp.int32)] * RING
        + [
            pltpu.SMEM(send_counts.shape, jnp.int32),
            pltpu.VMEM((rows, half), BF16),
            pltpu.VMEM((rows, half), F32),
            pltpu.VMEM((PEERS_STEP * slots, half), F32),
            pltpu.VMEM((peers, slots, half), BF16),
            pltpu.SemaphoreType.DMA((LOAD_PARTS,)),
            pltpu.SemaphoreType.DMA((RING,)),
            pltpu.SemaphoreType.DMA,
            pltpu.SemaphoreType.DMA((peers // PEERS_STEP,)),
        ],
        compiler_params=pltpu.CompilerParams(vmem_limit_bytes=12 * 2**20),
        name="pick_rows",
    )(in_hbm(send_rows), in_hbm(send_counts), in_hbm(own))


def adjacency_kernel(core_ref, codes_ref, out_ref):
    per_tile, edges = codes_ref.shape[1:]
    ids = lax.broadcasted_iota(jnp.int32, (TILE, edges), 0).astype(F32).astype(BF16)
    one = jnp.ones((TILE, edges), BF16)
    zero = jnp.zeros((TILE, edges), BF16)

    def hot(values):
        spread = jnp.broadcast_to(values.astype(F32), (16, edges)).astype(BF16)
        spread = jnp.concatenate([spread] * (TILE // 16), axis=0)
        return jnp.where(spread == ids, one, zero).astype(F8)

    for q in range(PAIR):
        for k in range(per_tile):
            codes = codes_ref[q, k : k + 1, :]
            counts = lax.dot_general(
                hot(codes >> 7),
                hot(codes & (TILE - 1)),
                (((1,), (1,)), ((), ())),
                preferred_element_type=F32,
            )
            out_ref[q, :, k * TILE : (k + 1) * TILE] = counts.astype(BF16)


def adjacency(core, codes, tiles):
    _, per_tile, edges = codes.shape
    steps = tiles // PAIR
    return pl.pallas_call(
        adjacency_kernel,
        grid_spec=pltpu.PrefetchScalarGridSpec(
            num_scalar_prefetch=1,
            grid=(steps,),
            in_specs=[
                pl.BlockSpec(
                    (PAIR, per_tile, edges), lambda t, core_ref: (core_ref[0] * steps + t, 0, 0)
                )
            ],
            out_specs=pl.BlockSpec((PAIR, TILE, per_tile * TILE), lambda t, core_ref: (t, 0, 0)),
        ),
        out_shape=pltpu.HBM((tiles, TILE, per_tile * TILE), BF16),
        compiler_params=params(12),
        cost_estimate=pl.CostEstimate(
            flops=2 * tiles * per_tile * TILE * TILE * edges * 2,
            transcendentals=0,
            bytes_accessed=tiles * per_tile * (TILE * TILE * 2 + edges * 4),
        ),
        name="adjacency",
    )(core, in_hbm(codes))


def stage_kernel(own_ref, mine_ref, adj_ref, near_ref, early_ref, sems):
    own_tiles = own_ref.shape[0]
    copies = [
        pltpu.make_async_copy(own_ref, near_ref.at[pl.ds(0, own_tiles)], sems.at[0]),
        pltpu.make_async_copy(
            mine_ref, near_ref.at[pl.ds(own_tiles, mine_ref.shape[0])], sems.at[1]
        ),
    ]
    for t in range(early_ref.shape[0]):
        copies.append(pltpu.make_async_copy(adj_ref.at[t], early_ref.at[t], sems.at[2 + t]))
    for copy in copies:
        copy.start()
    for copy in copies:
        copy.wait()


def stage(own, mine, adj):
    early = adj.shape[0] // 2
    source_tiles = own.shape[0] + mine.shape[0]
    return pl.pallas_call(
        stage_kernel,
        in_specs=[
            pl.BlockSpec(memory_space=pl.ANY),
            pl.BlockSpec(memory_space=pl.ANY),
            pl.BlockSpec(memory_space=pltpu.HBM),
        ],
        out_specs=[pl.BlockSpec(memory_space=pltpu.VMEM)] * 2,
        out_shape=[
            jax.ShapeDtypeStruct((source_tiles,) + own.shape[1:], BF16),
            jax.ShapeDtypeStruct((early,) + adj.shape[1:], BF16),
        ],
        scratch_shapes=[pltpu.SemaphoreType.DMA((2 + early,))],
        compiler_params=pltpu.CompilerParams(vmem_limit_bytes=2 * 2**20),
        name="stage",
    )(own, mine, in_hbm(adj))


def aggregate_kernel(
    core_ref,
    tile_src_ref,
    adj_ref,
    deg_ref,
    weight_ref,
    other_ref,
    sibling_ref,
    near,
    early,
    keep_ref,
    send_ref,
    keep_stats_ref,
    send_stats_ref,
    far,
    late,
    sems,
):
    per_tile = tile_src_ref.shape[1]
    own_tiles, _, half = other_ref.shape
    peers = sibling_ref.shape[0]
    tiles = adj_ref.shape[0]
    ahead = early.shape[0]
    core = core_ref[0]

    def late_copy(t):
        return pltpu.make_async_copy(adj_ref.at[ahead + t], late.at[t], sems.at[2 + t])

    copies = [
        pltpu.make_async_copy(other_ref, far.at[pl.ds(0, own_tiles)], sems.at[0]),
        pltpu.make_async_copy(sibling_ref, far.at[pl.ds(own_tiles, peers)], sems.at[1]),
    ]
    for copy in copies:
        copy.start()
    for t in range(tiles - ahead):
        late_copy(t).start()
    for copy in copies:
        copy.wait()

    def source(number):
        return jnp.concatenate([near[number], far[number]], axis=1)

    def block(counts, base, at):
        inputs = []
        for q in range(TILES_STEP):
            row = core * tiles + base + at + q
            total = jnp.zeros((TILE, 2 * half), F32)
            for k in range(0, per_tile, 2):
                pair = jnp.concatenate(
                    [source(tile_src_ref[row, k]), source(tile_src_ref[row, k + 1])], axis=0
                )
                total += jnp.dot(
                    counts[at + q, :, k * TILE : (k + 2) * TILE],
                    pair,
                    preferred_element_type=F32,
                )
            degree = jnp.broadcast_to(deg_ref[row].astype(F32), (8, TILE)).T[:, :1]
            inputs.append(jnp.concatenate([source(row), (total / degree).astype(BF16)], axis=1))
        pre = jnp.dot(
            jnp.concatenate(inputs, axis=0), weight_ref[...], preferred_element_type=F32
        )
        rows = TILES_STEP * TILE
        here = pl.ds(pl.multiple_of((base + at) * TILE, rows), rows)
        keep_ref[here, :] = pre[:, :half]
        send_ref[here, :] = pre[:, half:]

    def early_step(step, carry):
        block(early, 0, step * TILES_STEP)
        return carry

    def late_step(step, carry):
        for q in range(TILES_STEP):
            late_copy(step * TILES_STEP + q).wait()
        block(late, ahead, step * TILES_STEP)
        return carry

    lax.fori_loop(0, ahead // TILES_STEP, early_step, 0)
    lax.fori_loop(0, (tiles - ahead) // TILES_STEP, late_step, 0)
    for values_ref, stats_ref in ((keep_ref, keep_stats_ref), (send_ref, send_stats_ref)):
        values = values_ref[...]
        sums = jnp.sum(values, axis=0, keepdims=True)
        centred = values - sums / values.shape[0]
        stats_ref[0:1, :] = sums
        stats_ref[1:2, :] = jnp.sum(centred * centred, axis=0, keepdims=True)


def aggregate(core, tile_src, adj, degrees, weights, other, sibling, near, early):
    tiles = adj.shape[0]
    late = tiles - early.shape[0]
    half = sibling.shape[2]
    rows = tiles * TILE
    smem = pl.BlockSpec(memory_space=pltpu.SMEM)
    vmem = pl.BlockSpec(memory_space=pltpu.VMEM)
    anywhere = pl.BlockSpec(memory_space=pl.ANY)
    hbm = pl.BlockSpec(memory_space=pltpu.HBM)
    return pl.pallas_call(
        aggregate_kernel,
        in_specs=[smem, smem, hbm, vmem, vmem, anywhere, anywhere, vmem, vmem],
        out_specs=[vmem] * 4,
        out_shape=[jax.ShapeDtypeStruct((rows, half), F32)] * 2
        + [jax.ShapeDtypeStruct((2, half), F32)] * 2,
        scratch_shapes=[
            pltpu.VMEM(near.shape, BF16),
            pltpu.VMEM((late,) + adj.shape[1:], BF16),
            pltpu.SemaphoreType.DMA((2 + late,)),
        ],
        compiler_params=pltpu.CompilerParams(vmem_limit_bytes=20 * 2**20),
        name="aggregate",
    )(core, tile_src, in_hbm(adj), degrees, weights, other, sibling, near, early)


def normalise_kernel(core_ref, keep_ref, got_ref, parts_ref, gamma_ref, beta_ref, out_ref):
    rows = keep_ref.shape[0]
    parts = parts_ref[...]
    members = 2.0 * parts.shape[0]
    sums = jnp.concatenate([parts[:, 0, :], parts[:, 2, :]], axis=0)
    spreads = jnp.concatenate([parts[:, 1, :], parts[:, 3, :]], axis=0)
    mean = jnp.sum(sums, axis=0, keepdims=True) / (rows * members)
    shift = sums / rows - mean
    var = jnp.sum(spreads + rows * (shift * shift), axis=0, keepdims=True) / (rows * members)
    scale = gamma_ref[...] / jnp.sqrt(var + EPS)
    beta = beta_ref[...]
    here = pl.multiple_of(core_ref[0] * rows, rows)
    there = pl.multiple_of((1 - core_ref[0]) * rows, rows)
    out_ref[pl.ds(here, rows), :] = jnp.maximum(
        (keep_ref[...] - mean) * scale + beta, 0.0
    ).astype(BF16)
    out_ref[pl.ds(there, rows), :] = jnp.maximum(
        (got_ref[...] - mean) * scale + beta, 0.0
    ).astype(BF16)


def normalise(core, keep, got, parts, gamma, beta):
    rows, half = keep.shape
    whole = pl.BlockSpec(memory_space=pltpu.VMEM)
    return pl.pallas_call(
        normalise_kernel,
        in_specs=[pl.BlockSpec(memory_space=pltpu.SMEM)] + [whole] * 5,
        out_specs=whole,
        out_shape=jax.ShapeDtypeStruct((2 * rows, half), BF16),
        compiler_params=pltpu.CompilerParams(vmem_limit_bytes=8 * 2**20),
        name="normalise",
    )(core, keep, got, parts, gamma.reshape(1, half), beta.reshape(1, half))


def local(
    features, send_rows, send_counts, tile_src, edge_codes, degrees, w_self, w_neigh, gamma, beta
):
    rows, half = features.shape
    peers = lax.axis_size("dom")
    tiles = rows // TILE // 2
    core = lax.axis_index("feat").astype(jnp.int32)
    core_arg = core.reshape(1)
    swap = [(0, 1), (1, 0)]

    outgoing = pick_rows(send_rows, send_counts, features)
    mine = lax.all_to_all(outgoing, "dom", split_axis=0, concat_axis=0, tiled=True)
    other = lax.ppermute(features, "feat", swap)
    adj = adjacency(core_arg, edge_codes, tiles)

    def turned(w):
        return jnp.where(core == 0, w, jnp.roll(w, (half, half), (0, 1)))

    weights = jnp.concatenate([turned(w_self), turned(w_neigh)], axis=0)
    mine, adj, other, weights = lax.optimization_barrier((mine, adj, other, weights))
    sibling = lax.ppermute(mine, "feat", swap)
    other = other.reshape(-1, TILE, half)
    near, early = stage(features.reshape(-1, TILE, half), mine, adj)
    keep, send, keep_stats, send_stats = aggregate(
        core_arg,
        tile_src,
        adj,
        degrees.reshape(-1, 1, TILE),
        weights,
        other,
        sibling,
        near,
        early,
    )
    got_stats = lax.ppermute(send_stats, "feat", swap)
    got_stats, send = lax.optimization_barrier((got_stats, send))
    got = lax.ppermute(send, "feat", swap)
    stats = jnp.concatenate([keep_stats, got_stats], axis=0)
    stats = jnp.broadcast_to(stats[None], (peers,) + stats.shape)
    parts = lax.all_to_all(stats, "dom", split_axis=0, concat_axis=0, tiled=True)
    return normalise(core_arg, keep, got, parts, gamma, beta)


def solution(mesh):
    return jax.shard_map(
        local,
        mesh=mesh,
        in_specs=(
            P("dom", "feat"),
            P("dom", None, None),
            P("dom", None),
            P("dom", None),
            P("dom", None, None),
            P("dom"),
            P(),
            P(),
            P("feat"),
            P("feat"),
        ),
        out_specs=P("dom", "feat"),
        check_vma=False,
    )
```

```python
import jax
import jax.numpy as jnp
from jax import lax
from jax.experimental import pallas as pl
from jax.experimental.pallas import tpu as pltpu
from jax.sharding import PartitionSpec as P

TILE = 128
PEERS_STEP = 4
RING = 4
TILES_STEP = 4
PAIR = 2
LOAD_PARTS = 4
EPS = 1e-05
BF16 = jnp.bfloat16
F32 = jnp.float32
F8 = jnp.float8_e4m3fn


def params(mib, axes=1):
    return pltpu.CompilerParams(
        dimension_semantics=("arbitrary",) * axes, vmem_limit_bytes=mib * 2**20
    )


def in_hbm(array):
    return pltpu.with_memory_space_constraint(array, pltpu.HBM)


def in_vmem(array):
    return pltpu.with_memory_space_constraint(array, pltpu.VMEM)


def pick_kernel(rows_ref, counts_ref, own_ref, out_ref, *scratch):
    ring = scratch[:RING]
    counts, loaded, table, lines, done, own_sems, ring_sems, count_sem, out_sems = scratch[RING:]
    peers, slots, half = out_ref.shape
    part = own_ref.shape[0] // LOAD_PARTS
    rounds = peers // (PEERS_STEP * RING)

    def row_copy(g, b):
        wanted = rows_ref.at[0, pl.ds(g * PEERS_STEP, PEERS_STEP)]
        return pltpu.make_async_copy(wanted, ring[b], ring_sems.at[b])

    def out_copy(g):
        at = pl.ds(g * PEERS_STEP, PEERS_STEP)
        return pltpu.make_async_copy(done.at[at], out_ref.at[at], out_sems.at[g])

    count_copy = pltpu.make_async_copy(counts_ref, counts, count_sem)
    own_copies = [
        pltpu.make_async_copy(
            own_ref.at[pl.ds(q * part, part)], loaded.at[pl.ds(q * part, part)], own_sems.at[q]
        )
        for q in range(LOAD_PARTS)
    ]
    for b in range(RING):
        row_copy(b, b).start()
    count_copy.start()
    for copy in own_copies:
        copy.start()
    for q, copy in enumerate(own_copies):
        copy.wait()
        table[q * part : (q + 1) * part, :] = loaded[q * part : (q + 1) * part, :].astype(F32)
    count_copy.wait()
    slot = lax.broadcasted_iota(jnp.int32, (slots, half), 0)

    def one_round(i, carry):
        for b in range(RING):
            g = i * RING + b
            row_copy(g, b).wait()
            for p in range(PEERS_STEP):
                for s in range(slots):
                    at = p * slots + s
                    lines[at : at + 1, :] = table[pl.ds(ring[b][p, s], 1), :]

            @pl.when(i < rounds - 1)
            def _():
                row_copy(g + RING, b).start()

            for p in range(PEERS_STEP):
                peer = g * PEERS_STEP + p
                block = lines[p * slots : (p + 1) * slots, :]
                done[peer] = jnp.where(slot < counts[0, peer], block, 0.0).astype(BF16)
            out_copy(g).start()
        return carry

    def finish(g, carry):
        out_copy(g).wait()
        return carry

    lax.fori_loop(0, rounds, one_round, 0)
    lax.fori_loop(0, peers // PEERS_STEP, finish, 0)


def pick_rows(send_rows, send_counts, own):
    _, peers, slots = send_rows.shape
    rows, half = own.shape
    hbm = pl.BlockSpec(memory_space=pltpu.HBM)
    return pl.pallas_call(
        pick_kernel,
        in_specs=[hbm, hbm, hbm],
        out_specs=hbm,
        out_shape=pltpu.HBM((peers, slots, half), BF16),
        scratch_shapes=[pltpu.SMEM((PEERS_STEP, slots), jnp.int32)] * RING
        + [
            pltpu.SMEM(send_counts.shape, jnp.int32),
            pltpu.VMEM((rows, half), BF16),
            pltpu.VMEM((rows, half), F32),
            pltpu.VMEM((PEERS_STEP * slots, half), F32),
            pltpu.VMEM((peers, slots, half), BF16),
            pltpu.SemaphoreType.DMA((LOAD_PARTS,)),
            pltpu.SemaphoreType.DMA((RING,)),
            pltpu.SemaphoreType.DMA,
            pltpu.SemaphoreType.DMA((peers // PEERS_STEP,)),
        ],
        compiler_params=pltpu.CompilerParams(vmem_limit_bytes=12 * 2**20),
        name="pick_rows",
    )(in_hbm(send_rows), in_hbm(send_counts), in_hbm(own))


def adjacency_kernel(core_ref, codes_ref, out_ref):
    per_tile, edges = codes_ref.shape[1:]
    ids = lax.broadcasted_iota(jnp.int32, (TILE, edges), 0).astype(F32).astype(BF16)
    one = jnp.ones((TILE, edges), BF16)
    zero = jnp.zeros((TILE, edges), BF16)

    def hot(values):
        spread = jnp.broadcast_to(values.astype(F32), (16, edges)).astype(BF16)
        spread = jnp.concatenate([spread] * (TILE // 16), axis=0)
        return jnp.where(spread == ids, one, zero).astype(F8)

    for q in range(PAIR):
        for k in range(per_tile):
            codes = codes_ref[q, k : k + 1, :]
            counts = lax.dot_general(
                hot(codes >> 7),
                hot(codes & (TILE - 1)),
                (((1,), (1,)), ((), ())),
                preferred_element_type=F32,
            )
            out_ref[q, :, k * TILE : (k + 1) * TILE] = counts.astype(BF16)


def adjacency(core, codes, tiles):
    _, per_tile, edges = codes.shape
    steps = tiles // PAIR
    return pl.pallas_call(
        adjacency_kernel,
        grid_spec=pltpu.PrefetchScalarGridSpec(
            num_scalar_prefetch=1,
            grid=(steps,),
            in_specs=[
                pl.BlockSpec(
                    (PAIR, per_tile, edges), lambda t, core_ref: (core_ref[0] * steps + t, 0, 0)
                )
            ],
            out_specs=pl.BlockSpec((PAIR, TILE, per_tile * TILE), lambda t, core_ref: (t, 0, 0)),
        ),
        out_shape=pltpu.HBM((tiles, TILE, per_tile * TILE), BF16),
        compiler_params=params(12),
        cost_estimate=pl.CostEstimate(
            flops=2 * tiles * per_tile * TILE * TILE * edges * 2,
            transcendentals=0,
            bytes_accessed=tiles * per_tile * (TILE * TILE * 2 + edges * 4),
        ),
        name="adjacency",
    )(core, in_hbm(codes))


def stage_kernel(adj_ref, staged_ref, sems):
    copies = [
        pltpu.make_async_copy(adj_ref.at[t], staged_ref.at[t], sems.at[t])
        for t in range(adj_ref.shape[0])
    ]
    for copy in copies:
        copy.start()
    for copy in copies:
        copy.wait()


def stage(adj, after):
    def kernel(adj_ref, after_ref, staged_ref, sems):
        stage_kernel(adj_ref, staged_ref, sems)

    return pl.pallas_call(
        kernel,
        in_specs=[
            pl.BlockSpec(memory_space=pltpu.HBM),
            pl.BlockSpec(memory_space=pl.ANY),
        ],
        out_specs=pl.BlockSpec(memory_space=pltpu.VMEM),
        out_shape=jax.ShapeDtypeStruct(adj.shape, adj.dtype),
        scratch_shapes=[pltpu.SemaphoreType.DMA((adj.shape[0],))],
        compiler_params=pltpu.CompilerParams(vmem_limit_bytes=2 * 2**20),
        name="stage",
    )(in_hbm(adj), after)


def aggregate_kernel(
    core_ref,
    tile_src_ref,
    adj_ref,
    deg_ref,
    weight_ref,
    own_ref,
    other_ref,
    mine_ref,
    sibling_ref,
    keep_ref,
    send_ref,
    keep_stats_ref,
    send_stats_ref,
):
    per_tile = tile_src_ref.shape[1]
    own_tiles, _, half = other_ref.shape
    tiles = adj_ref.shape[0]
    core = core_ref[0]

    def source(number):
        owned = jnp.minimum(number, own_tiles - 1)
        halo = jnp.maximum(number - own_tiles, 0)
        is_own = number < own_tiles
        near = jnp.where(is_own, own_ref[owned], mine_ref[halo])
        far = jnp.where(is_own, other_ref[owned], sibling_ref[halo])
        return jnp.concatenate([near, far], axis=1)

    def block(step, carry):
        inputs = []
        for q in range(TILES_STEP):
            at = step * TILES_STEP + q
            row = core * tiles + at
            total = jnp.zeros((TILE, 2 * half), F32)
            for k in range(0, per_tile, 2):
                pair = jnp.concatenate(
                    [source(tile_src_ref[row, k]), source(tile_src_ref[row, k + 1])], axis=0
                )
                total += jnp.dot(
                    adj_ref[at, :, k * TILE : (k + 2) * TILE], pair, preferred_element_type=F32
                )
            degree = jnp.broadcast_to(deg_ref[row].astype(F32), (8, TILE)).T[:, :1]
            self_rows = jnp.concatenate([own_ref[row], other_ref[row]], axis=1)
            inputs.append(jnp.concatenate([self_rows, (total / degree).astype(BF16)], axis=1))
        pre = jnp.dot(
            jnp.concatenate(inputs, axis=0), weight_ref[...], preferred_element_type=F32
        )
        rows = TILES_STEP * TILE
        here = pl.ds(pl.multiple_of(step * rows, rows), rows)
        keep_ref[here, :] = pre[:, :half]
        send_ref[here, :] = pre[:, half:]
        return carry

    lax.fori_loop(0, tiles // TILES_STEP, block, 0)
    for values_ref, stats_ref in ((keep_ref, keep_stats_ref), (send_ref, send_stats_ref)):
        values = values_ref[...]
        sums = jnp.sum(values, axis=0, keepdims=True)
        centred = values - sums / values.shape[0]
        stats_ref[0:1, :] = sums
        stats_ref[1:2, :] = jnp.sum(centred * centred, axis=0, keepdims=True)


def aggregate(core, tile_src, adj, degrees, weights, own, other, mine, sibling):
    half = sibling.shape[2]
    rows = adj.shape[0] * TILE
    smem = pl.BlockSpec(memory_space=pltpu.SMEM)
    vmem = pl.BlockSpec(memory_space=pltpu.VMEM)
    return pl.pallas_call(
        aggregate_kernel,
        in_specs=[smem, smem] + [vmem] * 7,
        out_specs=[vmem] * 4,
        out_shape=[jax.ShapeDtypeStruct((rows, half), F32)] * 2
        + [jax.ShapeDtypeStruct((2, half), F32)] * 2,
        compiler_params=pltpu.CompilerParams(vmem_limit_bytes=8 * 2**20),
        name="aggregate",
    )(core, tile_src, adj, degrees, weights, own, other, mine, in_vmem(sibling))


def normalise_kernel(core_ref, keep_ref, got_ref, parts_ref, gamma_ref, beta_ref, out_ref):
    rows = keep_ref.shape[0]
    parts = parts_ref[...]
    members = 2.0 * parts.shape[0]
    sums = jnp.concatenate([parts[:, 0, :], parts[:, 2, :]], axis=0)
    spreads = jnp.concatenate([parts[:, 1, :], parts[:, 3, :]], axis=0)
    mean = jnp.sum(sums, axis=0, keepdims=True) / (rows * members)
    shift = sums / rows - mean
    var = jnp.sum(spreads + rows * (shift * shift), axis=0, keepdims=True) / (rows * members)
    scale = gamma_ref[...] / jnp.sqrt(var + EPS)
    beta = beta_ref[...]
    here = pl.multiple_of(core_ref[0] * rows, rows)
    there = pl.multiple_of((1 - core_ref[0]) * rows, rows)
    out_ref[pl.ds(here, rows), :] = jnp.maximum(
        (keep_ref[...] - mean) * scale + beta, 0.0
    ).astype(BF16)
    out_ref[pl.ds(there, rows), :] = jnp.maximum(
        (got_ref[...] - mean) * scale + beta, 0.0
    ).astype(BF16)


def normalise(core, keep, got, parts, gamma, beta):
    rows, half = keep.shape
    whole = pl.BlockSpec(memory_space=pltpu.VMEM)
    return pl.pallas_call(
        normalise_kernel,
        in_specs=[pl.BlockSpec(memory_space=pltpu.SMEM)] + [whole] * 5,
        out_specs=whole,
        out_shape=jax.ShapeDtypeStruct((2 * rows, half), BF16),
        compiler_params=pltpu.CompilerParams(vmem_limit_bytes=8 * 2**20),
        name="normalise",
    )(core, keep, got, parts, gamma.reshape(1, half), beta.reshape(1, half))


def local(
    features, send_rows, send_counts, tile_src, edge_codes, degrees, w_self, w_neigh, gamma, beta
):
    rows, half = features.shape
    peers = lax.axis_size("dom")
    tiles = rows // TILE // 2
    core = lax.axis_index("feat").astype(jnp.int32)
    core_arg = core.reshape(1)
    swap = [(0, 1), (1, 0)]

    outgoing = pick_rows(send_rows, send_counts, features)
    mine = lax.all_to_all(outgoing, "dom", split_axis=0, concat_axis=0, tiled=True)
    other = lax.ppermute(features, "feat", swap)
    adj = adjacency(core_arg, edge_codes, tiles)

    def turned(w):
        return jnp.where(core == 0, w, jnp.roll(w, (half, half), (0, 1)))

    weights = jnp.concatenate([turned(w_self), turned(w_neigh)], axis=0)
    mine, adj, other, weights = lax.optimization_barrier((mine, adj, other, weights))
    sibling = lax.ppermute(mine, "feat", swap)
    other = other.reshape(-1, TILE, half)
    keep, send, keep_stats, send_stats = aggregate(
        core_arg,
        tile_src,
        stage(adj, mine),
        degrees.reshape(-1, 1, TILE),
        weights,
        features.reshape(-1, TILE, half),
        other,
        mine,
        sibling,
    )
    got_stats = lax.ppermute(send_stats, "feat", swap)
    got_stats, send = lax.optimization_barrier((got_stats, send))
    got = lax.ppermute(send, "feat", swap)
    stats = jnp.concatenate([keep_stats, got_stats], axis=0)
    stats = jnp.broadcast_to(stats[None], (peers,) + stats.shape)
    parts = lax.all_to_all(stats, "dom", split_axis=0, concat_axis=0, tiled=True)
    return normalise(core_arg, keep, got, parts, gamma, beta)


def solution(mesh):
    return jax.shard_map(
        local,
        mesh=mesh,
        in_specs=(
            P("dom", "feat"),
            P("dom", None, None),
            P("dom", None),
            P("dom", None),
            P("dom", None, None),
            P("dom"),
            P(),
            P(),
            P("feat"),
            P("feat"),
        ),
        out_specs=P("dom", "feat"),
        check_vma=False,
    )
```

```python
import jax
import jax.numpy as jnp
from jax import lax
from jax.experimental import pallas as pl
from jax.experimental.pallas import tpu as pltpu
from jax.sharding import PartitionSpec as P

TILE = 128
PEERS_STEP = 4
RING = 4
TILES_STEP = 4
PAIR = 2
LOAD_PARTS = 4
EPS = 1e-05
BF16 = jnp.bfloat16
F32 = jnp.float32
F8 = jnp.float8_e4m3fn


def params(mib, axes=1):
    return pltpu.CompilerParams(
        dimension_semantics=("arbitrary",) * axes, vmem_limit_bytes=mib * 2**20
    )


def in_hbm(array):
    return pltpu.with_memory_space_constraint(array, pltpu.HBM)


def pick_kernel(rows_ref, counts_ref, own_ref, out_ref, *scratch):
    ring = scratch[:RING]
    counts, loaded, table, lines, done, own_sems, ring_sems, count_sem, out_sems = scratch[RING:]
    peers, slots, half = out_ref.shape
    part = own_ref.shape[0] // LOAD_PARTS
    rounds = peers // (PEERS_STEP * RING)

    def row_copy(g, b):
        wanted = rows_ref.at[0, pl.ds(g * PEERS_STEP, PEERS_STEP)]
        return pltpu.make_async_copy(wanted, ring[b], ring_sems.at[b])

    def out_copy(g):
        at = pl.ds(g * PEERS_STEP, PEERS_STEP)
        return pltpu.make_async_copy(done.at[at], out_ref.at[at], out_sems.at[g])

    count_copy = pltpu.make_async_copy(counts_ref, counts, count_sem)
    own_copies = [
        pltpu.make_async_copy(
            own_ref.at[pl.ds(q * part, part)], loaded.at[pl.ds(q * part, part)], own_sems.at[q]
        )
        for q in range(LOAD_PARTS)
    ]
    for b in range(RING):
        row_copy(b, b).start()
    count_copy.start()
    for copy in own_copies:
        copy.start()
    for q, copy in enumerate(own_copies):
        copy.wait()
        table[q * part : (q + 1) * part, :] = loaded[q * part : (q + 1) * part, :].astype(F32)
    count_copy.wait()
    slot = lax.broadcasted_iota(jnp.int32, (slots, half), 0)

    def one_round(i, carry):
        for b in range(RING):
            g = i * RING + b
            row_copy(g, b).wait()
            for p in range(PEERS_STEP):
                for s in range(slots):
                    at = p * slots + s
                    lines[at : at + 1, :] = table[pl.ds(ring[b][p, s], 1), :]

            @pl.when(i < rounds - 1)
            def _():
                row_copy(g + RING, b).start()

            for p in range(PEERS_STEP):
                peer = g * PEERS_STEP + p
                block = lines[p * slots : (p + 1) * slots, :]
                done[peer] = jnp.where(slot < counts[0, peer], block, 0.0).astype(BF16)
            out_copy(g).start()
        return carry

    def finish(g, carry):
        out_copy(g).wait()
        return carry

    lax.fori_loop(0, rounds, one_round, 0)
    lax.fori_loop(0, peers // PEERS_STEP, finish, 0)


def pick_rows(send_rows, send_counts, own):
    _, peers, slots = send_rows.shape
    rows, half = own.shape
    hbm = pl.BlockSpec(memory_space=pltpu.HBM)
    return pl.pallas_call(
        pick_kernel,
        in_specs=[hbm, hbm, hbm],
        out_specs=hbm,
        out_shape=pltpu.HBM((peers, slots, half), BF16),
        scratch_shapes=[pltpu.SMEM((PEERS_STEP, slots), jnp.int32)] * RING
        + [
            pltpu.SMEM(send_counts.shape, jnp.int32),
            pltpu.VMEM((rows, half), BF16),
            pltpu.VMEM((rows, half), F32),
            pltpu.VMEM((PEERS_STEP * slots, half), F32),
            pltpu.VMEM((peers, slots, half), BF16),
            pltpu.SemaphoreType.DMA((LOAD_PARTS,)),
            pltpu.SemaphoreType.DMA((RING,)),
            pltpu.SemaphoreType.DMA,
            pltpu.SemaphoreType.DMA((peers // PEERS_STEP,)),
        ],
        compiler_params=pltpu.CompilerParams(vmem_limit_bytes=12 * 2**20),
        name="pick_rows",
    )(in_hbm(send_rows), in_hbm(send_counts), in_hbm(own))


def adjacency_kernel(core_ref, codes_ref, out_ref):
    per_tile, edges = codes_ref.shape[1:]
    ids = lax.broadcasted_iota(jnp.int32, (TILE, edges), 0).astype(F32).astype(BF16)
    one = jnp.ones((TILE, edges), BF16)
    zero = jnp.zeros((TILE, edges), BF16)

    def hot(values):
        spread = jnp.broadcast_to(values.astype(F32), (16, edges)).astype(BF16)
        spread = jnp.concatenate([spread] * (TILE // 16), axis=0)
        return jnp.where(spread == ids, one, zero).astype(F8)

    for q in range(PAIR):
        for k in range(per_tile):
            codes = codes_ref[q, k : k + 1, :]
            counts = lax.dot_general(
                hot(codes >> 7),
                hot(codes & (TILE - 1)),
                (((1,), (1,)), ((), ())),
                preferred_element_type=F32,
            )
            out_ref[q, :, k * TILE : (k + 1) * TILE] = counts.astype(BF16)


def adjacency(core, codes, tiles):
    _, per_tile, edges = codes.shape
    steps = tiles // PAIR
    return pl.pallas_call(
        adjacency_kernel,
        grid_spec=pltpu.PrefetchScalarGridSpec(
            num_scalar_prefetch=1,
            grid=(steps,),
            in_specs=[
                pl.BlockSpec(
                    (PAIR, per_tile, edges), lambda t, core_ref: (core_ref[0] * steps + t, 0, 0)
                )
            ],
            out_specs=pl.BlockSpec((PAIR, TILE, per_tile * TILE), lambda t, core_ref: (t, 0, 0)),
        ),
        out_shape=pltpu.HBM((tiles, TILE, per_tile * TILE), BF16),
        compiler_params=params(12),
        cost_estimate=pl.CostEstimate(
            flops=2 * tiles * per_tile * TILE * TILE * edges * 2,
            transcendentals=0,
            bytes_accessed=tiles * per_tile * (TILE * TILE * 2 + edges * 4),
        ),
        name="adjacency",
    )(core, in_hbm(codes))


def stage_kernel(own_ref, mine_ref, adj_ref, near_ref, early_ref, sems):
    own_tiles = own_ref.shape[0]
    copies = [
        pltpu.make_async_copy(own_ref, near_ref.at[pl.ds(0, own_tiles)], sems.at[0]),
        pltpu.make_async_copy(
            mine_ref, near_ref.at[pl.ds(own_tiles, mine_ref.shape[0])], sems.at[1]
        ),
    ]
    for t in range(early_ref.shape[0]):
        copies.append(pltpu.make_async_copy(adj_ref.at[t], early_ref.at[t], sems.at[2 + t]))
    for copy in copies:
        copy.start()
    for copy in copies:
        copy.wait()


def stage(own, mine, adj):
    early = adj.shape[0] // 2
    source_tiles = own.shape[0] + mine.shape[0]
    return pl.pallas_call(
        stage_kernel,
        in_specs=[
            pl.BlockSpec(memory_space=pl.ANY),
            pl.BlockSpec(memory_space=pl.ANY),
            pl.BlockSpec(memory_space=pltpu.HBM),
        ],
        out_specs=[pl.BlockSpec(memory_space=pltpu.VMEM)] * 2,
        out_shape=[
            jax.ShapeDtypeStruct((source_tiles,) + own.shape[1:], BF16),
            jax.ShapeDtypeStruct((early,) + adj.shape[1:], BF16),
        ],
        scratch_shapes=[pltpu.SemaphoreType.DMA((2 + early,))],
        compiler_params=pltpu.CompilerParams(vmem_limit_bytes=2 * 2**20),
        name="stage",
    )(own, mine, in_hbm(adj))


def aggregate_kernel(
    core_ref,
    tile_src_ref,
    adj_ref,
    deg_ref,
    weight_ref,
    other_ref,
    sibling_ref,
    near,
    early,
    keep_ref,
    send_ref,
    keep_stats_ref,
    send_stats_ref,
    far,
    late,
    sems,
):
    per_tile = tile_src_ref.shape[1]
    own_tiles, _, half = other_ref.shape
    peers = sibling_ref.shape[0]
    tiles = adj_ref.shape[0]
    ahead = early.shape[0]
    core = core_ref[0]

    def late_copy(t):
        return pltpu.make_async_copy(adj_ref.at[ahead + t], late.at[t], sems.at[2 + t])

    copies = [
        pltpu.make_async_copy(other_ref, far.at[pl.ds(0, own_tiles)], sems.at[0]),
        pltpu.make_async_copy(sibling_ref, far.at[pl.ds(own_tiles, peers)], sems.at[1]),
    ]
    for copy in copies:
        copy.start()
    for copy in copies:
        copy.wait()
    for t in range(tiles - ahead):
        late_copy(t).start()

    def source(number):
        return jnp.concatenate([near[number], far[number]], axis=1)

    def block(counts, base, at, sums):
        inputs = []
        for q in range(TILES_STEP):
            row = core * tiles + base + at + q
            total = jnp.zeros((TILE, 2 * half), F32)
            for k in range(0, per_tile, 2):
                pair = jnp.concatenate(
                    [source(tile_src_ref[row, k]), source(tile_src_ref[row, k + 1])], axis=0
                )
                total += jnp.dot(
                    counts[at + q, :, k * TILE : (k + 2) * TILE],
                    pair,
                    preferred_element_type=F32,
                )
            degree = jnp.broadcast_to(deg_ref[row].astype(F32), (8, TILE)).T[:, :1]
            inputs.append(jnp.concatenate([source(row), (total / degree).astype(BF16)], axis=1))
        pre = jnp.dot(
            jnp.concatenate(inputs, axis=0), weight_ref[...], preferred_element_type=F32
        )
        rows = TILES_STEP * TILE
        here = pl.ds(pl.multiple_of((base + at) * TILE, rows), rows)
        keep_ref[here, :] = pre[:, :half]
        send_ref[here, :] = pre[:, half:]
        return sums + jnp.sum(pre, axis=0, keepdims=True)

    def early_step(step, sums):
        return block(early, 0, step * TILES_STEP, sums)

    def late_step(step, sums):
        for q in range(TILES_STEP):
            late_copy(step * TILES_STEP + q).wait()
        return block(late, ahead, step * TILES_STEP, sums)

    sums = jnp.zeros((1, 2 * half), F32)
    sums = lax.fori_loop(0, ahead // TILES_STEP, early_step, sums)
    sums = lax.fori_loop(0, (tiles - ahead) // TILES_STEP, late_step, sums)
    for values_ref, stats_ref, total in (
        (keep_ref, keep_stats_ref, sums[:, :half]),
        (send_ref, send_stats_ref, sums[:, half:]),
    ):
        centred = values_ref[...] - total / values_ref.shape[0]
        stats_ref[0:1, :] = total
        stats_ref[1:2, :] = jnp.sum(centred * centred, axis=0, keepdims=True)


def aggregate(core, tile_src, adj, degrees, weights, other, sibling, near, early):
    tiles = adj.shape[0]
    late = tiles - early.shape[0]
    half = sibling.shape[2]
    rows = tiles * TILE
    smem = pl.BlockSpec(memory_space=pltpu.SMEM)
    vmem = pl.BlockSpec(memory_space=pltpu.VMEM)
    anywhere = pl.BlockSpec(memory_space=pl.ANY)
    hbm = pl.BlockSpec(memory_space=pltpu.HBM)
    return pl.pallas_call(
        aggregate_kernel,
        in_specs=[smem, smem, hbm, vmem, vmem, anywhere, anywhere, vmem, vmem],
        out_specs=[vmem] * 4,
        out_shape=[jax.ShapeDtypeStruct((rows, half), F32)] * 2
        + [jax.ShapeDtypeStruct((2, half), F32)] * 2,
        scratch_shapes=[
            pltpu.VMEM(near.shape, BF16),
            pltpu.VMEM((late,) + adj.shape[1:], BF16),
            pltpu.SemaphoreType.DMA((2 + late,)),
        ],
        compiler_params=pltpu.CompilerParams(vmem_limit_bytes=12 * 2**20),
        name="aggregate",
    )(core, tile_src, in_hbm(adj), degrees, weights, other, sibling, near, early)


def normalise_kernel(core_ref, keep_ref, got_ref, parts_ref, gamma_ref, beta_ref, out_ref):
    rows = keep_ref.shape[0]
    parts = parts_ref[...]
    members = 2.0 * parts.shape[0]
    sums = jnp.concatenate([parts[:, 0, :], parts[:, 2, :]], axis=0)
    spreads = jnp.concatenate([parts[:, 1, :], parts[:, 3, :]], axis=0)
    mean = jnp.sum(sums, axis=0, keepdims=True) / (rows * members)
    shift = sums / rows - mean
    var = jnp.sum(spreads + rows * (shift * shift), axis=0, keepdims=True) / (rows * members)
    scale = gamma_ref[...] / jnp.sqrt(var + EPS)
    beta = beta_ref[...]
    here = pl.multiple_of(core_ref[0] * rows, rows)
    there = pl.multiple_of((1 - core_ref[0]) * rows, rows)
    out_ref[pl.ds(here, rows), :] = jnp.maximum(
        (keep_ref[...] - mean) * scale + beta, 0.0
    ).astype(BF16)
    out_ref[pl.ds(there, rows), :] = jnp.maximum(
        (got_ref[...] - mean) * scale + beta, 0.0
    ).astype(BF16)


def normalise(core, keep, got, parts, gamma, beta):
    rows, half = keep.shape
    whole = pl.BlockSpec(memory_space=pltpu.VMEM)
    return pl.pallas_call(
        normalise_kernel,
        in_specs=[pl.BlockSpec(memory_space=pltpu.SMEM)] + [whole] * 5,
        out_specs=whole,
        out_shape=jax.ShapeDtypeStruct((2 * rows, half), BF16),
        compiler_params=pltpu.CompilerParams(vmem_limit_bytes=8 * 2**20),
        name="normalise",
    )(core, keep, got, parts, gamma.reshape(1, half), beta.reshape(1, half))


def local(
    features, send_rows, send_counts, tile_src, edge_codes, degrees, w_self, w_neigh, gamma, beta
):
    rows, half = features.shape
    peers = lax.axis_size("dom")
    tiles = rows // TILE // 2
    core = lax.axis_index("feat").astype(jnp.int32)
    core_arg = core.reshape(1)
    swap = [(0, 1), (1, 0)]

    outgoing = pick_rows(send_rows, send_counts, features)
    mine = lax.all_to_all(outgoing, "dom", split_axis=0, concat_axis=0, tiled=True)
    other = lax.ppermute(features, "feat", swap)
    adj = adjacency(core_arg, edge_codes, tiles)

    def turned(w):
        return jnp.where(core == 0, w, jnp.roll(w, (half, half), (0, 1)))

    weights = jnp.concatenate([turned(w_self), turned(w_neigh)], axis=0)
    mine, adj, other, weights = lax.optimization_barrier((mine, adj, other, weights))
    sibling = lax.ppermute(mine, "feat", swap)
    other = other.reshape(-1, TILE, half)
    near, early = stage(features.reshape(-1, TILE, half), in_hbm(mine), adj)
    keep, send, keep_stats, send_stats = aggregate(
        core_arg,
        tile_src,
        adj,
        degrees.reshape(-1, 1, TILE),
        weights,
        other,
        sibling,
        near,
        early,
    )
    got_stats = lax.ppermute(send_stats, "feat", swap)
    got_stats, send = lax.optimization_barrier((got_stats, send))
    got = lax.ppermute(send, "feat", swap)
    stats = jnp.concatenate([keep_stats, got_stats], axis=0)
    stats = jnp.broadcast_to(stats[None], (peers,) + stats.shape)
    parts = lax.all_to_all(stats, "dom", split_axis=0, concat_axis=0, tiled=True)
    return normalise(core_arg, keep, got, parts, gamma, beta)


def solution(mesh):
    return jax.shard_map(
        local,
        mesh=mesh,
        in_specs=(
            P("dom", "feat"),
            P("dom", None, None),
            P("dom", None),
            P("dom", None),
            P("dom", None, None),
            P("dom"),
            P(),
            P(),
            P("feat"),
            P("feat"),
        ),
        out_specs=P("dom", "feat"),
        check_vma=False,
    )
```

```python
import jax
import jax.numpy as jnp
from jax import lax
from jax.experimental import pallas as pl
from jax.experimental.pallas import tpu as pltpu
from jax.sharding import PartitionSpec as P

TILE = 128
PEERS_STEP = 4
RING = 4
TILES_STEP = 4
PAIR = 2
OUT_PARTS = 4
LOAD_PARTS = 4
EPS = 1e-05
BF16 = jnp.bfloat16
F32 = jnp.float32
F8 = jnp.float8_e4m3fn


def params(mib, axes=1):
    return pltpu.CompilerParams(
        dimension_semantics=("arbitrary",) * axes, vmem_limit_bytes=mib * 2**20
    )


def in_hbm(array):
    return pltpu.with_memory_space_constraint(array, pltpu.HBM)


def pick_kernel(rows_ref, counts_ref, own_ref, out_ref, *scratch):
    ring = scratch[:RING]
    counts, loaded, table, lines, done, own_sems, ring_sems, count_sem, out_sems = scratch[RING:]
    peers, slots, half = out_ref.shape
    part = own_ref.shape[0] // LOAD_PARTS
    rounds = peers // (PEERS_STEP * RING)

    def row_copy(g, b):
        wanted = rows_ref.at[0, pl.ds(g * PEERS_STEP, PEERS_STEP)]
        return pltpu.make_async_copy(wanted, ring[b], ring_sems.at[b])

    def out_copy(g):
        at = pl.ds(g * PEERS_STEP, PEERS_STEP)
        return pltpu.make_async_copy(done.at[at], out_ref.at[at], out_sems.at[g])

    count_copy = pltpu.make_async_copy(counts_ref, counts, count_sem)
    own_copies = [
        pltpu.make_async_copy(
            own_ref.at[pl.ds(q * part, part)], loaded.at[pl.ds(q * part, part)], own_sems.at[q]
        )
        for q in range(LOAD_PARTS)
    ]
    for b in range(RING):
        row_copy(b, b).start()
    count_copy.start()
    for copy in own_copies:
        copy.start()
    for q, copy in enumerate(own_copies):
        copy.wait()
        table[q * part : (q + 1) * part, :] = loaded[q * part : (q + 1) * part, :].astype(F32)
    count_copy.wait()
    slot = lax.broadcasted_iota(jnp.int32, (slots, half), 0)

    def one_round(i, carry):
        for b in range(RING):
            g = i * RING + b
            row_copy(g, b).wait()
            for p in range(PEERS_STEP):
                for s in range(slots):
                    at = p * slots + s
                    lines[at : at + 1, :] = table[pl.ds(ring[b][p, s], 1), :]

            @pl.when(i < rounds - 1)
            def _():
                row_copy(g + RING, b).start()

            for p in range(PEERS_STEP):
                peer = g * PEERS_STEP + p
                block = lines[p * slots : (p + 1) * slots, :]
                done[peer] = jnp.where(slot < counts[0, peer], block, 0.0).astype(BF16)
            out_copy(g).start()
        return carry

    def finish(g, carry):
        out_copy(g).wait()
        return carry

    lax.fori_loop(0, rounds, one_round, 0)
    lax.fori_loop(0, peers // PEERS_STEP, finish, 0)


def pick_rows(send_rows, send_counts, own):
    _, peers, slots = send_rows.shape
    rows, half = own.shape
    hbm = pl.BlockSpec(memory_space=pltpu.HBM)
    return pl.pallas_call(
        pick_kernel,
        in_specs=[hbm, hbm, hbm],
        out_specs=hbm,
        out_shape=pltpu.HBM((peers, slots, half), BF16),
        scratch_shapes=[pltpu.SMEM((PEERS_STEP, slots), jnp.int32)] * RING
        + [
            pltpu.SMEM(send_counts.shape, jnp.int32),
            pltpu.VMEM((rows, half), BF16),
            pltpu.VMEM((rows, half), F32),
            pltpu.VMEM((PEERS_STEP * slots, half), F32),
            pltpu.VMEM((peers, slots, half), BF16),
            pltpu.SemaphoreType.DMA((LOAD_PARTS,)),
            pltpu.SemaphoreType.DMA((RING,)),
            pltpu.SemaphoreType.DMA,
            pltpu.SemaphoreType.DMA((peers // PEERS_STEP,)),
        ],
        compiler_params=pltpu.CompilerParams(vmem_limit_bytes=12 * 2**20),
        name="pick_rows",
    )(in_hbm(send_rows), in_hbm(send_counts), in_hbm(own))


def adjacency_kernel(core_ref, codes_ref, out_ref):
    per_tile, edges = codes_ref.shape[1:]
    ids = lax.broadcasted_iota(jnp.int32, (TILE, edges), 0).astype(F32).astype(BF16)
    one = jnp.ones((TILE, edges), BF16)
    zero = jnp.zeros((TILE, edges), BF16)

    def hot(values):
        spread = jnp.broadcast_to(values.astype(F32), (16, edges)).astype(BF16)
        spread = jnp.concatenate([spread] * (TILE // 16), axis=0)
        return jnp.where(spread == ids, one, zero).astype(F8)

    for q in range(PAIR):
        for k in range(per_tile):
            codes = codes_ref[q, k : k + 1, :]
            counts = lax.dot_general(
                hot(codes >> 7),
                hot(codes & (TILE - 1)),
                (((1,), (1,)), ((), ())),
                preferred_element_type=F32,
            )
            out_ref[q, :, k * TILE : (k + 1) * TILE] = counts.astype(BF16)


def adjacency(core, codes, tiles):
    _, per_tile, edges = codes.shape
    steps = tiles // PAIR
    return pl.pallas_call(
        adjacency_kernel,
        grid_spec=pltpu.PrefetchScalarGridSpec(
            num_scalar_prefetch=1,
            grid=(steps,),
            in_specs=[
                pl.BlockSpec(
                    (PAIR, per_tile, edges), lambda t, core_ref: (core_ref[0] * steps + t, 0, 0)
                )
            ],
            out_specs=pl.BlockSpec((PAIR, TILE, per_tile * TILE), lambda t, core_ref: (t, 0, 0)),
        ),
        out_shape=pltpu.HBM((tiles, TILE, per_tile * TILE), BF16),
        compiler_params=params(12),
        cost_estimate=pl.CostEstimate(
            flops=2 * tiles * per_tile * TILE * TILE * edges * 2,
            transcendentals=0,
            bytes_accessed=tiles * per_tile * (TILE * TILE * 2 + edges * 4),
        ),
        name="adjacency",
    )(core, in_hbm(codes))


def stage_kernel(own_ref, mine_ref, adj_ref, near_ref, early_ref, sems):
    own_tiles = own_ref.shape[0]
    copies = [
        pltpu.make_async_copy(own_ref, near_ref.at[pl.ds(0, own_tiles)], sems.at[0]),
        pltpu.make_async_copy(
            mine_ref, near_ref.at[pl.ds(own_tiles, mine_ref.shape[0])], sems.at[1]
        ),
    ]
    for t in range(early_ref.shape[0]):
        copies.append(pltpu.make_async_copy(adj_ref.at[t], early_ref.at[t], sems.at[2 + t]))
    for copy in copies:
        copy.start()
    for copy in copies:
        copy.wait()


def stage(own, mine, adj):
    early = adj.shape[0] // 2
    source_tiles = own.shape[0] + mine.shape[0]
    return pl.pallas_call(
        stage_kernel,
        in_specs=[
            pl.BlockSpec(memory_space=pl.ANY),
            pl.BlockSpec(memory_space=pl.ANY),
            pl.BlockSpec(memory_space=pltpu.HBM),
        ],
        out_specs=[pl.BlockSpec(memory_space=pltpu.VMEM)] * 2,
        out_shape=[
            jax.ShapeDtypeStruct((source_tiles,) + own.shape[1:], BF16),
            jax.ShapeDtypeStruct((early,) + adj.shape[1:], BF16),
        ],
        scratch_shapes=[pltpu.SemaphoreType.DMA((2 + early,))],
        compiler_params=pltpu.CompilerParams(vmem_limit_bytes=2 * 2**20),
        name="stage",
    )(own, mine, in_hbm(adj))


def aggregate_kernel(
    core_ref,
    tile_src_ref,
    adj_ref,
    deg_ref,
    weight_ref,
    other_ref,
    sibling_ref,
    near,
    early,
    keep_ref,
    send_ref,
    keep_stats_ref,
    send_stats_ref,
    far,
    late,
    sems,
):
    per_tile = tile_src_ref.shape[1]
    own_tiles, _, half = other_ref.shape
    peers = sibling_ref.shape[0]
    tiles = adj_ref.shape[0]
    ahead = early.shape[0]
    core = core_ref[0]

    def late_copy(t):
        return pltpu.make_async_copy(adj_ref.at[ahead + t], late.at[t], sems.at[2 + t])

    copies = [
        pltpu.make_async_copy(other_ref, far.at[pl.ds(0, own_tiles)], sems.at[0]),
        pltpu.make_async_copy(sibling_ref, far.at[pl.ds(own_tiles, peers)], sems.at[1]),
    ]
    for copy in copies:
        copy.start()
    for copy in copies:
        copy.wait()
    for t in range(tiles - ahead):
        late_copy(t).start()

    def source(number):
        return jnp.concatenate([near[number], far[number]], axis=1)

    def block(counts, base, at, sums):
        inputs = []
        for q in range(TILES_STEP):
            row = core * tiles + base + at + q
            total = jnp.zeros((TILE, 2 * half), F32)
            for k in range(0, per_tile, 2):
                pair = jnp.concatenate(
                    [source(tile_src_ref[row, k]), source(tile_src_ref[row, k + 1])], axis=0
                )
                total += jnp.dot(
                    counts[at + q, :, k * TILE : (k + 2) * TILE],
                    pair,
                    preferred_element_type=F32,
                )
            degree = jnp.broadcast_to(deg_ref[row].astype(F32), (8, TILE)).T[:, :1]
            inputs.append(jnp.concatenate([source(row), (total / degree).astype(BF16)], axis=1))
        pre = jnp.dot(
            jnp.concatenate(inputs, axis=0), weight_ref[...], preferred_element_type=F32
        )
        rows = TILES_STEP * TILE
        here = pl.ds(pl.multiple_of((base + at) * TILE, rows), rows)
        keep_ref[here, :] = pre[:, :half]
        send_ref[here, :] = pre[:, half:]
        return sums + jnp.sum(pre, axis=0, keepdims=True)

    def early_step(step, sums):
        return block(early, 0, step * TILES_STEP, sums)

    def late_step(step, sums):
        for q in range(TILES_STEP):
            late_copy(step * TILES_STEP + q).wait()
        return block(late, ahead, step * TILES_STEP, sums)

    sums = jnp.zeros((1, 2 * half), F32)
    sums = lax.fori_loop(0, ahead // TILES_STEP, early_step, sums)
    sums = lax.fori_loop(0, (tiles - ahead) // TILES_STEP, late_step, sums)
    for values_ref, stats_ref, total in (
        (keep_ref, keep_stats_ref, sums[:, :half]),
        (send_ref, send_stats_ref, sums[:, half:]),
    ):
        centred = values_ref[...] - total / values_ref.shape[0]
        stats_ref[0:1, :] = total
        stats_ref[1:2, :] = jnp.sum(centred * centred, axis=0, keepdims=True)


def aggregate(core, tile_src, adj, degrees, weights, other, sibling, near, early):
    tiles = adj.shape[0]
    late = tiles - early.shape[0]
    half = sibling.shape[2]
    rows = tiles * TILE
    smem = pl.BlockSpec(memory_space=pltpu.SMEM)
    vmem = pl.BlockSpec(memory_space=pltpu.VMEM)
    anywhere = pl.BlockSpec(memory_space=pl.ANY)
    hbm = pl.BlockSpec(memory_space=pltpu.HBM)
    return pl.pallas_call(
        aggregate_kernel,
        in_specs=[smem, smem, hbm, vmem, vmem, anywhere, anywhere, vmem, vmem],
        out_specs=[vmem] * 4,
        out_shape=[jax.ShapeDtypeStruct((rows, half), F32)] * 2
        + [jax.ShapeDtypeStruct((2, half), F32)] * 2,
        scratch_shapes=[
            pltpu.VMEM(near.shape, BF16),
            pltpu.VMEM((late,) + adj.shape[1:], BF16),
            pltpu.SemaphoreType.DMA((2 + late,)),
        ],
        compiler_params=pltpu.CompilerParams(vmem_limit_bytes=12 * 2**20),
        name="aggregate",
    )(core, tile_src, in_hbm(adj), degrees, weights, other, sibling, near, early)


def normalise_kernel(
    core_ref, keep_ref, got_ref, parts_ref, gamma_ref, beta_ref, out_ref, done, sems
):
    rows = keep_ref.shape[0]
    count = 2.0 * rows
    parts = parts_ref[...]
    members = parts.shape[0]
    sums = parts[:, 0, :]
    mean = jnp.sum(sums, axis=0, keepdims=True) / (count * members)
    shift = sums / count - mean
    spreads = parts[:, 1, :] + count * (shift * shift)
    var = jnp.sum(spreads, axis=0, keepdims=True) / (count * members)
    scale = gamma_ref[...] / jnp.sqrt(var + EPS)
    beta = beta_ref[...]
    size = rows // OUT_PARTS
    copies = []
    for values_ref, core in ((keep_ref, core_ref[0]), (got_ref, 1 - core_ref[0])):
        for q in range(OUT_PARTS):
            n = len(copies)
            values = (values_ref[q * size : (q + 1) * size, :] - mean) * scale + beta
            done[n] = jnp.maximum(values, 0.0).astype(BF16)
            at = pl.ds(pl.multiple_of(core * rows + q * size, size), size)
            copies.append(pltpu.make_async_copy(done.at[n], out_ref.at[at, :], sems.at[n]))
            copies[n].start()
    for copy in copies:
        copy.wait()


def normalise(core, keep, got, parts, gamma, beta):
    rows, half = keep.shape
    whole = pl.BlockSpec(memory_space=pltpu.VMEM)
    return pl.pallas_call(
        normalise_kernel,
        in_specs=[pl.BlockSpec(memory_space=pltpu.SMEM)] + [whole] * 5,
        out_specs=pl.BlockSpec(memory_space=pltpu.HBM),
        out_shape=jax.ShapeDtypeStruct((2 * rows, half), BF16),
        scratch_shapes=[
            pltpu.VMEM((2 * OUT_PARTS, rows // OUT_PARTS, half), BF16),
            pltpu.SemaphoreType.DMA((2 * OUT_PARTS,)),
        ],
        compiler_params=pltpu.CompilerParams(vmem_limit_bytes=8 * 2**20),
        name="normalise",
    )(core, keep, got, parts, gamma.reshape(1, half), beta.reshape(1, half))


def local(
    features, send_rows, send_counts, tile_src, edge_codes, degrees, w_self, w_neigh, gamma, beta
):
    rows, half = features.shape
    peers = lax.axis_size("dom")
    tiles = rows // TILE // 2
    core = lax.axis_index("feat").astype(jnp.int32)
    core_arg = core.reshape(1)
    swap = [(0, 1), (1, 0)]

    outgoing = pick_rows(send_rows, send_counts, features)
    mine = lax.all_to_all(outgoing, "dom", split_axis=0, concat_axis=0, tiled=True)
    adj = adjacency(core_arg, edge_codes, tiles)
    late_features, adj = lax.optimization_barrier((features, adj))
    other = lax.ppermute(late_features, "feat", swap)

    def turned(w):
        return jnp.where(core == 0, w, jnp.roll(w, (half, half), (0, 1)))

    weights = jnp.concatenate([turned(w_self), turned(w_neigh)], axis=0)
    mine, adj, other, weights = lax.optimization_barrier((mine, adj, other, weights))
    sibling = lax.ppermute(mine, "feat", swap)
    other = other.reshape(-1, TILE, half)
    near, early = stage(features.reshape(-1, TILE, half), in_hbm(mine), adj)
    keep, send, keep_stats, send_stats = aggregate(
        core_arg,
        tile_src,
        adj,
        degrees.reshape(-1, 1, TILE),
        weights,
        other,
        sibling,
        near,
        early,
    )
    got_stats = lax.ppermute(send_stats, "feat", swap)
    got_stats, send = lax.optimization_barrier((got_stats, send))
    got = lax.ppermute(send, "feat", swap)
    apart = keep_stats[0:1] - got_stats[0:1]
    both = keep_stats + got_stats
    spread = both[1:2] + apart * apart / (2.0 * keep.shape[0])
    stats = jnp.concatenate([both[0:1], spread], axis=0)
    stats = jnp.broadcast_to(stats[None], (peers,) + stats.shape)
    parts = lax.all_to_all(stats, "dom", split_axis=0, concat_axis=0, tiled=True)
    return normalise(core_arg, keep, got, parts, gamma, beta)


def solution(mesh):
    return jax.shard_map(
        local,
        mesh=mesh,
        in_specs=(
            P("dom", "feat"),
            P("dom", None, None),
            P("dom", None),
            P("dom", None),
            P("dom", None, None),
            P("dom"),
            P(),
            P(),
            P("feat"),
            P("feat"),
        ),
        out_specs=P("dom", "feat"),
        check_vma=False,
    )
```

```python
import jax
import jax.numpy as jnp
from jax import lax
from jax.experimental import pallas as pl
from jax.experimental.pallas import tpu as pltpu
from jax.sharding import PartitionSpec as P

TILE = 128
PEERS_STEP = 4
RING = 4
TILES_STEP = 4
PAIR = 2
OUT_PARTS = 4
LOAD_PARTS = 4
EPS = 1e-05
BF16 = jnp.bfloat16
F32 = jnp.float32
F8 = jnp.float8_e4m3fn


def params(mib, axes=1):
    return pltpu.CompilerParams(
        dimension_semantics=("arbitrary",) * axes, vmem_limit_bytes=mib * 2**20
    )


def in_hbm(array):
    return pltpu.with_memory_space_constraint(array, pltpu.HBM)


def pick_kernel(rows_ref, counts_ref, own_ref, out_ref, *scratch):
    ring = scratch[:RING]
    counts, loaded, table, lines, done, own_sems, ring_sems, count_sem, out_sems = scratch[RING:]
    peers, slots, half = out_ref.shape
    part = own_ref.shape[0] // LOAD_PARTS
    rounds = peers // (PEERS_STEP * RING)

    def row_copy(g, b):
        wanted = rows_ref.at[0, pl.ds(g * PEERS_STEP, PEERS_STEP)]
        return pltpu.make_async_copy(wanted, ring[b], ring_sems.at[b])

    def out_copy(g):
        at = pl.ds(g * PEERS_STEP, PEERS_STEP)
        return pltpu.make_async_copy(done.at[at], out_ref.at[at], out_sems.at[g])

    count_copy = pltpu.make_async_copy(counts_ref, counts, count_sem)
    own_copies = [
        pltpu.make_async_copy(
            own_ref.at[pl.ds(q * part, part)], loaded.at[pl.ds(q * part, part)], own_sems.at[q]
        )
        for q in range(LOAD_PARTS)
    ]
    for b in range(RING):
        row_copy(b, b).start()
    count_copy.start()
    for copy in own_copies:
        copy.start()
    for q, copy in enumerate(own_copies):
        copy.wait()
        table[q * part : (q + 1) * part, :] = loaded[q * part : (q + 1) * part, :].astype(F32)
    count_copy.wait()
    slot = lax.broadcasted_iota(jnp.int32, (slots, half), 0)

    def one_round(i, carry):
        for b in range(RING):
            g = i * RING + b
            row_copy(g, b).wait()
            for p in range(PEERS_STEP):
                for s in range(slots):
                    at = p * slots + s
                    lines[at : at + 1, :] = table[pl.ds(ring[b][p, s], 1), :]

            @pl.when(i < rounds - 1)
            def _():
                row_copy(g + RING, b).start()

            for p in range(PEERS_STEP):
                peer = g * PEERS_STEP + p
                block = lines[p * slots : (p + 1) * slots, :]
                done[peer] = jnp.where(slot < counts[0, peer], block, 0.0).astype(BF16)
            out_copy(g).start()
        return carry

    def finish(g, carry):
        out_copy(g).wait()
        return carry

    lax.fori_loop(0, rounds, one_round, 0)
    lax.fori_loop(0, peers // PEERS_STEP, finish, 0)


def pick_rows(send_rows, send_counts, own):
    _, peers, slots = send_rows.shape
    rows, half = own.shape
    hbm = pl.BlockSpec(memory_space=pltpu.HBM)
    return pl.pallas_call(
        pick_kernel,
        in_specs=[hbm, hbm, hbm],
        out_specs=hbm,
        out_shape=pltpu.HBM((peers, slots, half), BF16),
        scratch_shapes=[pltpu.SMEM((PEERS_STEP, slots), jnp.int32)] * RING
        + [
            pltpu.SMEM(send_counts.shape, jnp.int32),
            pltpu.VMEM((rows, half), BF16),
            pltpu.VMEM((rows, half), F32),
            pltpu.VMEM((PEERS_STEP * slots, half), F32),
            pltpu.VMEM((peers, slots, half), BF16),
            pltpu.SemaphoreType.DMA((LOAD_PARTS,)),
            pltpu.SemaphoreType.DMA((RING,)),
            pltpu.SemaphoreType.DMA,
            pltpu.SemaphoreType.DMA((peers // PEERS_STEP,)),
        ],
        compiler_params=pltpu.CompilerParams(vmem_limit_bytes=12 * 2**20),
        name="pick_rows",
    )(in_hbm(send_rows), in_hbm(send_counts), in_hbm(own))


def adjacency_kernel(core_ref, codes_ref, out_ref):
    per_tile, edges = codes_ref.shape[1:]
    ids = lax.broadcasted_iota(jnp.int32, (TILE, edges), 0).astype(F32).astype(BF16)
    one = jnp.ones((TILE, edges), BF16)
    zero = jnp.zeros((TILE, edges), BF16)

    def hot(values):
        spread = jnp.broadcast_to(values.astype(F32), (16, edges)).astype(BF16)
        spread = jnp.concatenate([spread] * (TILE // 16), axis=0)
        return jnp.where(spread == ids, one, zero).astype(F8)

    for q in range(PAIR):
        for k in range(per_tile):
            codes = codes_ref[q, k : k + 1, :]
            counts = lax.dot_general(
                hot(codes >> 7),
                hot(codes & (TILE - 1)),
                (((1,), (1,)), ((), ())),
                preferred_element_type=F32,
            )
            out_ref[q, :, k * TILE : (k + 1) * TILE] = counts.astype(BF16)


def adjacency(core, codes, tiles):
    _, per_tile, edges = codes.shape
    steps = tiles // PAIR
    return pl.pallas_call(
        adjacency_kernel,
        grid_spec=pltpu.PrefetchScalarGridSpec(
            num_scalar_prefetch=1,
            grid=(steps,),
            in_specs=[
                pl.BlockSpec(
                    (PAIR, per_tile, edges), lambda t, core_ref: (core_ref[0] * steps + t, 0, 0)
                )
            ],
            out_specs=pl.BlockSpec((PAIR, TILE, per_tile * TILE), lambda t, core_ref: (t, 0, 0)),
        ),
        out_shape=pltpu.HBM((tiles, TILE, per_tile * TILE), BF16),
        compiler_params=params(12),
        cost_estimate=pl.CostEstimate(
            flops=2 * tiles * per_tile * TILE * TILE * edges * 2,
            transcendentals=0,
            bytes_accessed=tiles * per_tile * (TILE * TILE * 2 + edges * 4),
        ),
        name="adjacency",
    )(core, in_hbm(codes))


def stage_kernel(own_ref, mine_ref, adj_ref, near_ref, early_ref, sems):
    own_tiles = own_ref.shape[0]
    copies = [
        pltpu.make_async_copy(own_ref, near_ref.at[pl.ds(0, own_tiles)], sems.at[0]),
        pltpu.make_async_copy(
            mine_ref, near_ref.at[pl.ds(own_tiles, mine_ref.shape[0])], sems.at[1]
        ),
    ]
    for t in range(early_ref.shape[0]):
        copies.append(pltpu.make_async_copy(adj_ref.at[t], early_ref.at[t], sems.at[2 + t]))
    for copy in copies:
        copy.start()
    for copy in copies:
        copy.wait()


def stage(own, mine, adj):
    early = adj.shape[0] // 2
    source_tiles = own.shape[0] + mine.shape[0]
    return pl.pallas_call(
        stage_kernel,
        in_specs=[
            pl.BlockSpec(memory_space=pl.ANY),
            pl.BlockSpec(memory_space=pl.ANY),
            pl.BlockSpec(memory_space=pltpu.HBM),
        ],
        out_specs=[pl.BlockSpec(memory_space=pltpu.VMEM)] * 2,
        out_shape=[
            jax.ShapeDtypeStruct((source_tiles,) + own.shape[1:], BF16),
            jax.ShapeDtypeStruct((early,) + adj.shape[1:], BF16),
        ],
        scratch_shapes=[pltpu.SemaphoreType.DMA((2 + early,))],
        compiler_params=pltpu.CompilerParams(vmem_limit_bytes=2 * 2**20),
        name="stage",
    )(own, mine, in_hbm(adj))


def aggregate_kernel(
    core_ref,
    tile_src_ref,
    adj_ref,
    deg_ref,
    weight_ref,
    other_ref,
    sibling_ref,
    near,
    early,
    keep_ref,
    send_ref,
    stats_ref,
    far,
    late,
    sems,
):
    per_tile = tile_src_ref.shape[1]
    own_tiles, _, half = other_ref.shape
    peers = sibling_ref.shape[0]
    tiles = adj_ref.shape[0]
    ahead = early.shape[0]
    core = core_ref[0]

    def late_copy(t):
        return pltpu.make_async_copy(adj_ref.at[ahead + t], late.at[t], sems.at[2 + t])

    copies = [
        pltpu.make_async_copy(other_ref, far.at[pl.ds(0, own_tiles)], sems.at[0]),
        pltpu.make_async_copy(sibling_ref, far.at[pl.ds(own_tiles, peers)], sems.at[1]),
    ]
    for copy in copies:
        copy.start()
    for copy in copies:
        copy.wait()
    for t in range(tiles - ahead):
        late_copy(t).start()

    def source(number):
        return jnp.concatenate([near[number], far[number]], axis=1)

    def block(counts, base, at, sums):
        inputs = []
        for q in range(TILES_STEP):
            row = core * tiles + base + at + q
            total = jnp.zeros((TILE, 2 * half), F32)
            for k in range(0, per_tile, 2):
                pair = jnp.concatenate(
                    [source(tile_src_ref[row, k]), source(tile_src_ref[row, k + 1])], axis=0
                )
                total += jnp.dot(
                    counts[at + q, :, k * TILE : (k + 2) * TILE],
                    pair,
                    preferred_element_type=F32,
                )
            degree = jnp.broadcast_to(deg_ref[row].astype(F32), (8, TILE)).T[:, :1]
            inputs.append(jnp.concatenate([source(row), (total / degree).astype(BF16)], axis=1))
        pre = jnp.dot(
            jnp.concatenate(inputs, axis=0), weight_ref[...], preferred_element_type=F32
        )
        rows = TILES_STEP * TILE
        here = pl.ds(pl.multiple_of((base + at) * TILE, rows), rows)
        keep_ref[here, :] = pre[:, :half]
        send_ref[here, :] = pre[:, half:]
        return sums + jnp.sum(pre, axis=0, keepdims=True)

    def early_step(step, sums):
        return block(early, 0, step * TILES_STEP, sums)

    def late_step(step, sums):
        for q in range(TILES_STEP):
            late_copy(step * TILES_STEP + q).wait()
        return block(late, ahead, step * TILES_STEP, sums)

    sums = jnp.zeros((1, 2 * half), F32)
    sums = lax.fori_loop(0, ahead // TILES_STEP, early_step, sums)
    sums = lax.fori_loop(0, (tiles - ahead) // TILES_STEP, late_step, sums)
    for values_ref, owner, total in (
        (keep_ref, core, sums[:, :half]),
        (send_ref, 1 - core, sums[:, half:]),
    ):
        centred = values_ref[...] - total / values_ref.shape[0]
        spread = jnp.sum(centred * centred, axis=0, keepdims=True)
        stats_ref[owner] = jnp.concatenate([total, spread], axis=0)


def aggregate(core, tile_src, adj, degrees, weights, other, sibling, near, early):
    tiles = adj.shape[0]
    late = tiles - early.shape[0]
    half = sibling.shape[2]
    rows = tiles * TILE
    smem = pl.BlockSpec(memory_space=pltpu.SMEM)
    vmem = pl.BlockSpec(memory_space=pltpu.VMEM)
    anywhere = pl.BlockSpec(memory_space=pl.ANY)
    hbm = pl.BlockSpec(memory_space=pltpu.HBM)
    return pl.pallas_call(
        aggregate_kernel,
        in_specs=[smem, smem, hbm, vmem, vmem, anywhere, anywhere, vmem, vmem],
        out_specs=[vmem] * 3,
        out_shape=[jax.ShapeDtypeStruct((rows, half), F32)] * 2
        + [jax.ShapeDtypeStruct((2, 2, half), F32)],
        scratch_shapes=[
            pltpu.VMEM(near.shape, BF16),
            pltpu.VMEM((late,) + adj.shape[1:], BF16),
            pltpu.SemaphoreType.DMA((2 + late,)),
        ],
        compiler_params=pltpu.CompilerParams(vmem_limit_bytes=12 * 2**20),
        name="aggregate",
    )(core, tile_src, in_hbm(adj), degrees, weights, other, sibling, near, early)


def normalise_kernel(
    core_ref, keep_ref, got_ref, parts_ref, gamma_ref, beta_ref, out_ref, done, sems
):
    rows = keep_ref.shape[0]
    count = float(rows)
    parts = parts_ref[...]
    members = parts.shape[0]
    sums = parts[:, 0, :]
    mean = jnp.sum(sums, axis=0, keepdims=True) / (count * members)
    shift = sums / count - mean
    spreads = parts[:, 1, :] + count * (shift * shift)
    var = jnp.sum(spreads, axis=0, keepdims=True) / (count * members)
    scale = gamma_ref[...] / jnp.sqrt(var + EPS)
    beta = beta_ref[...]
    size = rows // OUT_PARTS
    copies = []
    for values_ref, core in ((keep_ref, core_ref[0]), (got_ref, 1 - core_ref[0])):
        for q in range(OUT_PARTS):
            n = len(copies)
            values = (values_ref[q * size : (q + 1) * size, :] - mean) * scale + beta
            done[n] = jnp.maximum(values, 0.0).astype(BF16)
            at = pl.ds(pl.multiple_of(core * rows + q * size, size), size)
            copies.append(pltpu.make_async_copy(done.at[n], out_ref.at[at, :], sems.at[n]))
            copies[n].start()
    for copy in copies:
        copy.wait()


def normalise(core, keep, got, parts, gamma, beta):
    rows, half = keep.shape
    whole = pl.BlockSpec(memory_space=pltpu.VMEM)
    return pl.pallas_call(
        normalise_kernel,
        in_specs=[pl.BlockSpec(memory_space=pltpu.SMEM)] + [whole] * 5,
        out_specs=pl.BlockSpec(memory_space=pltpu.HBM),
        out_shape=jax.ShapeDtypeStruct((2 * rows, half), BF16),
        scratch_shapes=[
            pltpu.VMEM((2 * OUT_PARTS, rows // OUT_PARTS, half), BF16),
            pltpu.SemaphoreType.DMA((2 * OUT_PARTS,)),
        ],
        compiler_params=pltpu.CompilerParams(vmem_limit_bytes=8 * 2**20),
        name="normalise",
    )(core, keep, got, parts, gamma.reshape(1, half), beta.reshape(1, half))


def local(
    features, send_rows, send_counts, tile_src, edge_codes, degrees, w_self, w_neigh, gamma, beta
):
    rows, half = features.shape
    peers = lax.axis_size("dom")
    tiles = rows // TILE // 2
    core = lax.axis_index("feat").astype(jnp.int32)
    core_arg = core.reshape(1)
    swap = [(0, 1), (1, 0)]

    outgoing = pick_rows(send_rows, send_counts, features)
    mine = lax.all_to_all(outgoing, "dom", split_axis=0, concat_axis=0, tiled=True)
    adj = adjacency(core_arg, edge_codes, tiles)
    late_features, adj = lax.optimization_barrier((features, adj))
    other = lax.ppermute(late_features, "feat", swap)

    def turned(w):
        return jnp.where(core == 0, w, jnp.roll(w, (half, half), (0, 1)))

    weights = jnp.concatenate([turned(w_self), turned(w_neigh)], axis=0)
    mine, adj, other, weights = lax.optimization_barrier((mine, adj, other, weights))
    sibling = lax.ppermute(mine, "feat", swap)
    other = other.reshape(-1, TILE, half)
    near, early = stage(features.reshape(-1, TILE, half), in_hbm(mine), adj)
    keep, send, stats = aggregate(
        core_arg,
        tile_src,
        adj,
        degrees.reshape(-1, 1, TILE),
        weights,
        other,
        sibling,
        near,
        early,
    )
    got = lax.ppermute(send, "feat", swap)
    stats = jnp.broadcast_to(stats[None], (peers,) + stats.shape)
    stats = stats.reshape(2 * peers, 2, half)
    parts = lax.all_to_all(stats, ("dom", "feat"), split_axis=0, concat_axis=0, tiled=True)
    return normalise(core_arg, keep, got, parts, gamma, beta)


def solution(mesh):
    return jax.shard_map(
        local,
        mesh=mesh,
        in_specs=(
            P("dom", "feat"),
            P("dom", None, None),
            P("dom", None),
            P("dom", None),
            P("dom", None, None),
            P("dom"),
            P(),
            P(),
            P("feat"),
            P("feat"),
        ),
        out_specs=P("dom", "feat"),
        check_vma=False,
    )
```

```python
import jax
import jax.numpy as jnp
from jax import lax
from jax.experimental import pallas as pl
from jax.experimental.pallas import tpu as pltpu
from jax.sharding import PartitionSpec as P

TILE = 128
PEERS_STEP = 4
RING = 4
TILES_STEP = 4
PAIR = 2
OUT_PARTS = 4
LOAD_PARTS = 4
EPS = 1e-05
BF16 = jnp.bfloat16
F32 = jnp.float32
F8 = jnp.float8_e4m3fn


def params(mib, axes=1):
    return pltpu.CompilerParams(
        dimension_semantics=("arbitrary",) * axes, vmem_limit_bytes=mib * 2**20
    )


def in_hbm(array):
    return pltpu.with_memory_space_constraint(array, pltpu.HBM)


def pick_kernel(rows_ref, counts_ref, own_ref, out_ref, *scratch):
    ring = scratch[:RING]
    counts, loaded, table, lines, done, own_sems, ring_sems, count_sem, out_sems = scratch[RING:]
    peers, slots, half = out_ref.shape
    part = own_ref.shape[0] // LOAD_PARTS
    rounds = peers // (PEERS_STEP * RING)

    def row_copy(g, b):
        wanted = rows_ref.at[0, pl.ds(g * PEERS_STEP, PEERS_STEP)]
        return pltpu.make_async_copy(wanted, ring[b], ring_sems.at[b])

    def out_copy(g):
        at = pl.ds(g * PEERS_STEP, PEERS_STEP)
        return pltpu.make_async_copy(done.at[at], out_ref.at[at], out_sems.at[g])

    count_copy = pltpu.make_async_copy(counts_ref, counts, count_sem)
    own_copies = [
        pltpu.make_async_copy(
            own_ref.at[pl.ds(q * part, part)], loaded.at[pl.ds(q * part, part)], own_sems.at[q]
        )
        for q in range(LOAD_PARTS)
    ]
    for b in range(RING):
        row_copy(b, b).start()
    count_copy.start()
    for copy in own_copies:
        copy.start()
    for q, copy in enumerate(own_copies):
        copy.wait()
        table[q * part : (q + 1) * part, :] = loaded[q * part : (q + 1) * part, :].astype(F32)
    count_copy.wait()
    slot = lax.broadcasted_iota(jnp.int32, (slots, half), 0)

    def one_round(i, carry):
        for b in range(RING):
            g = i * RING + b
            row_copy(g, b).wait()
            for p in range(PEERS_STEP):
                for s in range(slots):
                    at = p * slots + s
                    lines[at : at + 1, :] = table[pl.ds(ring[b][p, s], 1), :]

            @pl.when(i < rounds - 1)
            def _():
                row_copy(g + RING, b).start()

            for p in range(PEERS_STEP):
                peer = g * PEERS_STEP + p
                block = lines[p * slots : (p + 1) * slots, :]
                done[peer] = jnp.where(slot < counts[0, peer], block, 0.0).astype(BF16)
            out_copy(g).start()
        return carry

    def finish(g, carry):
        out_copy(g).wait()
        return carry

    lax.fori_loop(0, rounds, one_round, 0)
    lax.fori_loop(0, peers // PEERS_STEP, finish, 0)


def pick_rows(send_rows, send_counts, own):
    _, peers, slots = send_rows.shape
    rows, half = own.shape
    hbm = pl.BlockSpec(memory_space=pltpu.HBM)
    return pl.pallas_call(
        pick_kernel,
        in_specs=[hbm, hbm, hbm],
        out_specs=hbm,
        out_shape=pltpu.HBM((peers, slots, half), BF16),
        scratch_shapes=[pltpu.SMEM((PEERS_STEP, slots), jnp.int32)] * RING
        + [
            pltpu.SMEM(send_counts.shape, jnp.int32),
            pltpu.VMEM((rows, half), BF16),
            pltpu.VMEM((rows, half), F32),
            pltpu.VMEM((PEERS_STEP * slots, half), F32),
            pltpu.VMEM((peers, slots, half), BF16),
            pltpu.SemaphoreType.DMA((LOAD_PARTS,)),
            pltpu.SemaphoreType.DMA((RING,)),
            pltpu.SemaphoreType.DMA,
            pltpu.SemaphoreType.DMA((peers // PEERS_STEP,)),
        ],
        compiler_params=pltpu.CompilerParams(vmem_limit_bytes=12 * 2**20),
        name="pick_rows",
    )(in_hbm(send_rows), in_hbm(send_counts), in_hbm(own))


def adjacency_kernel(core_ref, codes_ref, out_ref):
    per_tile, edges = codes_ref.shape[1:]
    ids = lax.broadcasted_iota(jnp.int32, (TILE, edges), 0).astype(F32).astype(BF16)
    one = jnp.ones((TILE, edges), BF16)
    zero = jnp.zeros((TILE, edges), BF16)

    def hot(values):
        spread = jnp.broadcast_to(values.astype(F32), (16, edges)).astype(BF16)
        spread = jnp.concatenate([spread] * (TILE // 16), axis=0)
        return jnp.where(spread == ids, one, zero).astype(F8)

    for q in range(PAIR):
        for k in range(per_tile):
            codes = codes_ref[q, k : k + 1, :]
            counts = lax.dot_general(
                hot(codes >> 7),
                hot(codes & (TILE - 1)),
                (((1,), (1,)), ((), ())),
                preferred_element_type=F32,
            )
            out_ref[q, :, k * TILE : (k + 1) * TILE] = counts.astype(BF16)


def adjacency(core, codes, tiles):
    _, per_tile, edges = codes.shape
    steps = tiles // PAIR
    return pl.pallas_call(
        adjacency_kernel,
        grid_spec=pltpu.PrefetchScalarGridSpec(
            num_scalar_prefetch=1,
            grid=(steps,),
            in_specs=[
                pl.BlockSpec(
                    (PAIR, per_tile, edges), lambda t, core_ref: (core_ref[0] * steps + t, 0, 0)
                )
            ],
            out_specs=pl.BlockSpec((PAIR, TILE, per_tile * TILE), lambda t, core_ref: (t, 0, 0)),
        ),
        out_shape=pltpu.HBM((tiles, TILE, per_tile * TILE), BF16),
        compiler_params=params(12),
        cost_estimate=pl.CostEstimate(
            flops=2 * tiles * per_tile * TILE * TILE * edges * 2,
            transcendentals=0,
            bytes_accessed=tiles * per_tile * (TILE * TILE * 2 + edges * 4),
        ),
        name="adjacency",
    )(core, in_hbm(codes))


def stage_kernel(own_ref, mine_ref, adj_ref, near_ref, early_ref, sems):
    own_tiles = own_ref.shape[0]
    copies = [
        pltpu.make_async_copy(own_ref, near_ref.at[pl.ds(0, own_tiles)], sems.at[0]),
        pltpu.make_async_copy(
            mine_ref, near_ref.at[pl.ds(own_tiles, mine_ref.shape[0])], sems.at[1]
        ),
    ]
    for t in range(early_ref.shape[0]):
        copies.append(pltpu.make_async_copy(adj_ref.at[t], early_ref.at[t], sems.at[2 + t]))
    for copy in copies:
        copy.start()
    for copy in copies:
        copy.wait()


def stage(own, mine, adj):
    early = adj.shape[0] // 2
    source_tiles = own.shape[0] + mine.shape[0]
    return pl.pallas_call(
        stage_kernel,
        in_specs=[
            pl.BlockSpec(memory_space=pl.ANY),
            pl.BlockSpec(memory_space=pl.ANY),
            pl.BlockSpec(memory_space=pltpu.HBM),
        ],
        out_specs=[pl.BlockSpec(memory_space=pltpu.VMEM)] * 2,
        out_shape=[
            jax.ShapeDtypeStruct((source_tiles,) + own.shape[1:], BF16),
            jax.ShapeDtypeStruct((early,) + adj.shape[1:], BF16),
        ],
        scratch_shapes=[pltpu.SemaphoreType.DMA((2 + early,))],
        compiler_params=pltpu.CompilerParams(vmem_limit_bytes=2 * 2**20),
        name="stage",
    )(own, mine, in_hbm(adj))


def aggregate_kernel(
    core_ref,
    tile_src_ref,
    adj_ref,
    deg_ref,
    weight_ref,
    other_ref,
    sibling_ref,
    near,
    early,
    keep_ref,
    send_ref,
    stats_ref,
    late,
    sems,
):
    per_tile = tile_src_ref.shape[1]
    own_tiles, _, half = other_ref.shape
    tiles = adj_ref.shape[0]
    ahead = early.shape[0]
    core = core_ref[0]

    def late_copy(t):
        return pltpu.make_async_copy(adj_ref.at[ahead + t], late.at[t], sems.at[2 + t])

    for t in range(tiles - ahead):
        late_copy(t).start()

    def source(number):
        far = jnp.where(
            number < own_tiles,
            other_ref[jnp.minimum(number, own_tiles - 1)],
            sibling_ref[jnp.maximum(number - own_tiles, 0)],
        )
        return jnp.concatenate([near[number], far], axis=1)

    def block(counts, base, at, sums):
        inputs = []
        for q in range(TILES_STEP):
            row = core * tiles + base + at + q
            total = jnp.zeros((TILE, 2 * half), F32)
            for k in range(0, per_tile, 2):
                pair = jnp.concatenate(
                    [source(tile_src_ref[row, k]), source(tile_src_ref[row, k + 1])], axis=0
                )
                total += jnp.dot(
                    counts[at + q, :, k * TILE : (k + 2) * TILE],
                    pair,
                    preferred_element_type=F32,
                )
            degree = jnp.broadcast_to(deg_ref[row].astype(F32), (8, TILE)).T[:, :1]
            inputs.append(jnp.concatenate([source(row), (total / degree).astype(BF16)], axis=1))
        pre = jnp.dot(
            jnp.concatenate(inputs, axis=0), weight_ref[...], preferred_element_type=F32
        )
        rows = TILES_STEP * TILE
        here = pl.ds(pl.multiple_of((base + at) * TILE, rows), rows)
        keep_ref[here, :] = pre[:, :half]
        send_ref[here, :] = pre[:, half:]
        return sums + jnp.sum(pre, axis=0, keepdims=True)

    def early_step(step, sums):
        return block(early, 0, step * TILES_STEP, sums)

    def late_step(step, sums):
        for q in range(TILES_STEP):
            late_copy(step * TILES_STEP + q).wait()
        return block(late, ahead, step * TILES_STEP, sums)

    sums = jnp.zeros((1, 2 * half), F32)
    sums = lax.fori_loop(0, ahead // TILES_STEP, early_step, sums)
    sums = lax.fori_loop(0, (tiles - ahead) // TILES_STEP, late_step, sums)
    for values_ref, owner, total in (
        (keep_ref, core, sums[:, :half]),
        (send_ref, 1 - core, sums[:, half:]),
    ):
        centred = values_ref[...] - total / values_ref.shape[0]
        spread = jnp.sum(centred * centred, axis=0, keepdims=True)
        stats_ref[owner] = jnp.concatenate([total, spread], axis=0)


def aggregate(core, tile_src, adj, degrees, weights, other, sibling, near, early):
    tiles = adj.shape[0]
    late = tiles - early.shape[0]
    half = sibling.shape[2]
    rows = tiles * TILE
    smem = pl.BlockSpec(memory_space=pltpu.SMEM)
    vmem = pl.BlockSpec(memory_space=pltpu.VMEM)
    hbm = pl.BlockSpec(memory_space=pltpu.HBM)
    return pl.pallas_call(
        aggregate_kernel,
        in_specs=[smem, smem, hbm, vmem, vmem, vmem, vmem, vmem, vmem],
        out_specs=[vmem] * 3,
        out_shape=[jax.ShapeDtypeStruct((rows, half), F32)] * 2
        + [jax.ShapeDtypeStruct((2, 2, half), F32)],
        scratch_shapes=[
            pltpu.VMEM((late,) + adj.shape[1:], BF16),
            pltpu.SemaphoreType.DMA((2 + late,)),
        ],
        compiler_params=pltpu.CompilerParams(vmem_limit_bytes=12 * 2**20),
        name="aggregate",
    )(core, tile_src, in_hbm(adj), degrees, weights, other, sibling, near, early)


def normalise_kernel(
    core_ref, keep_ref, got_ref, parts_ref, gamma_ref, beta_ref, out_ref, done, sems
):
    rows = keep_ref.shape[0]
    count = float(rows)
    parts = parts_ref[...]
    members = parts.shape[0]
    sums = parts[:, 0, :]
    mean = jnp.sum(sums, axis=0, keepdims=True) / (count * members)
    shift = sums / count - mean
    spreads = parts[:, 1, :] + count * (shift * shift)
    var = jnp.sum(spreads, axis=0, keepdims=True) / (count * members)
    scale = gamma_ref[...] / jnp.sqrt(var + EPS)
    beta = beta_ref[...]
    size = rows // OUT_PARTS
    copies = []
    for values_ref, core in ((keep_ref, core_ref[0]), (got_ref, 1 - core_ref[0])):
        for q in range(OUT_PARTS):
            n = len(copies)
            values = (values_ref[q * size : (q + 1) * size, :] - mean) * scale + beta
            done[n] = jnp.maximum(values, 0.0).astype(BF16)
            at = pl.ds(pl.multiple_of(core * rows + q * size, size), size)
            copies.append(pltpu.make_async_copy(done.at[n], out_ref.at[at, :], sems.at[n]))
            copies[n].start()
    for copy in copies:
        copy.wait()


def normalise(core, keep, got, parts, gamma, beta):
    rows, half = keep.shape
    whole = pl.BlockSpec(memory_space=pltpu.VMEM)
    return pl.pallas_call(
        normalise_kernel,
        in_specs=[pl.BlockSpec(memory_space=pltpu.SMEM)] + [whole] * 5,
        out_specs=pl.BlockSpec(memory_space=pltpu.HBM),
        out_shape=jax.ShapeDtypeStruct((2 * rows, half), BF16),
        scratch_shapes=[
            pltpu.VMEM((2 * OUT_PARTS, rows // OUT_PARTS, half), BF16),
            pltpu.SemaphoreType.DMA((2 * OUT_PARTS,)),
        ],
        compiler_params=pltpu.CompilerParams(vmem_limit_bytes=8 * 2**20),
        name="normalise",
    )(core, keep, got, parts, gamma.reshape(1, half), beta.reshape(1, half))


def local(
    features, send_rows, send_counts, tile_src, edge_codes, degrees, w_self, w_neigh, gamma, beta
):
    rows, half = features.shape
    peers = lax.axis_size("dom")
    tiles = rows // TILE // 2
    core = lax.axis_index("feat").astype(jnp.int32)
    core_arg = core.reshape(1)
    swap = [(0, 1), (1, 0)]

    outgoing = pick_rows(send_rows, send_counts, features)
    mine = lax.all_to_all(outgoing, "dom", split_axis=0, concat_axis=0, tiled=True)
    adj = adjacency(core_arg, edge_codes, tiles)
    late_features, adj = lax.optimization_barrier((features, adj))
    other = lax.ppermute(late_features, "feat", swap)

    def turned(w):
        return jnp.where(core == 0, w, jnp.roll(w, (half, half), (0, 1)))

    weights = jnp.concatenate([turned(w_self), turned(w_neigh)], axis=0)
    mine, adj, other, weights = lax.optimization_barrier((mine, adj, other, weights))
    sibling = lax.ppermute(mine, "feat", swap)
    other = other.reshape(-1, TILE, half)
    near, early = stage(features.reshape(-1, TILE, half), in_hbm(mine), adj)
    keep, send, stats = aggregate(
        core_arg,
        tile_src,
        adj,
        degrees.reshape(-1, 1, TILE),
        weights,
        other,
        sibling,
        near,
        early,
    )
    got = lax.ppermute(send, "feat", swap)
    stats = jnp.broadcast_to(stats[None], (peers,) + stats.shape)
    stats = stats.reshape(2 * peers, 2, half)
    parts = lax.all_to_all(stats, ("dom", "feat"), split_axis=0, concat_axis=0, tiled=True)
    return normalise(core_arg, keep, got, parts, gamma, beta)


def solution(mesh):
    return jax.shard_map(
        local,
        mesh=mesh,
        in_specs=(
            P("dom", "feat"),
            P("dom", None, None),
            P("dom", None),
            P("dom", None),
            P("dom", None, None),
            P("dom"),
            P(),
            P(),
            P("feat"),
            P("feat"),
        ),
        out_specs=P("dom", "feat"),
        check_vma=False,
    )
```
